256 devices in a mesh: dom: 32 (over y, z), feat: 8 (over x, core).
Axes of the slice: x: 4, y: 4, z: 8, core: 2. Of those that a mesh axis runs over, the one named last changes fastest.
Arguments:
- feats: bfloat16 [131072, 1024], P('dom', 'feat'), may hold values from -6 to 6
- projection: bfloat16 [1024, 512], P('feat'), may hold values from -0.1875 to 0.1875
- tiles: bfloat16 [8192, 4, 128, 128], P(('dom', 'feat')), may hold values from -0.25 to 0.25
- slot_owner: int32 [8192, 1], P(('dom', 'feat')), may hold values from 0 to 31; in each aligned block of 32 rows (0 to 31, 32 to 63, ...) at most 2 rows name the same one
- slot_block: int32 [8192, 1], P(('dom', 'feat')), may hold values from 0 to 3
- source_block: int32 [8192, 4], P(('dom', 'feat')), may hold values from 0 to 3
- counts: int32 [131072], P(('dom', 'feat')), may hold values from 1 to 4
- out_grad: bfloat16 [131072, 256], P(('dom', 'feat')), may hold values from -0.015625 to 0.015625
Outputs:
- activated: bfloat16 [131072, 256], P(('dom', 'feat'))
- weight_grad: float32 [1024, 512], P('feat')
The draws below stay inside these ranges and needn't reach their ends.
Inputs may be any that keep to these rules, and one draw needn't show every extreme that they name: `slot_owner`: among the 32 sent rows of one device, no dom index is named more than 2 times; some device names one exactly 2 times.
All inputs are finite; a program needn't handle non-finite values.
Results may differ from the reference program's by a relative error of at most 0.0059.
Values may be sent and summed in bfloat16 or wider, within the bound.
A program may use at most 128 MiB of HBM per device.

```python
import math
import jax
import jax.numpy as jnp
import numpy as np
from jax import lax

F = 1024
HID = 256
BLOCK = 128
BLK_DEV = 4
SLOTS_DEV = 32
KB = 4
CAP = 2
NODES = 131072
SLOTS = 8192
N_DOM = 32
N_FEAT = 8


def touch_ends(entries, key, low, high):
    spot = [jax.random.randint(jax.random.fold_in(key, axis), (), 0, length) for axis, length in enumerate(entries.shape)]
    longest = entries.shape.index(max(entries.shape))
    beside = spot[:longest] + [(spot[longest] + 1) % entries.shape[longest]] + spot[longest + 1:]
    return entries.at[tuple(spot)].set(low).at[tuple(beside)].set(high)


def level_of(rng, shape, cuts, least, largest):
    loudness, own = 1.0, jax.random.fold_in(rng, 6)
    for dim, parts in cuts:
        draws = jnp.exp(jax.random.uniform(jax.random.fold_in(own, dim), (parts,), jnp.float32, least / len(cuts), largest / len(cuts)))
        loudness = loudness * jnp.repeat(draws, shape[dim] // parts).reshape([-1 if axis == dim else 1 for axis in range(len(shape))])
    return loudness


def assign_block(rng, own, number, rows, count, top, most, skew):
    sequence = jax.random.permutation(rng, count)
    crowded, common = shares(count, rows * top, most, skew, True), shares(count, rows * top, most, skew, False)
    places = jnp.arange(count)

    def named(tallies, turn):
        used = int((tallies > 0).sum())
        fixed = max(1, used // 4)
        passed = fixed + (places - fixed + turn * (used - fixed)) % max(1, count - fixed)
        return jnp.zeros((count,), jnp.int32).at[sequence[jnp.where(places < fixed, places, passed)]].set(jnp.asarray(tallies, jnp.int32))

    tallies = jnp.where(number % 4 == 0, named(crowded, number // 4), named(common, number - number // 4 - 1))
    mixed = jax.random.permutation(jax.random.fold_in(own, 3), count)
    donor, sink = mixed[0:count // 2 * 2:2], mixed[1:count // 2 * 2:2]
    slack = jnp.minimum(tallies[donor] - 1, most - tallies[sink]) // 2
    slack = jnp.where((donor == sequence[0]) | (sink == sequence[0]) | (tallies[sink] == 0), 0, jnp.maximum(slack, 0))
    passed = jax.random.randint(jax.random.fold_in(own, 4), (count // 2,), 0, 1 << 20) % (slack + 1)
    tallies = tallies.at[donor].add(-passed).at[sink].add(passed)
    labels = jnp.searchsorted(jnp.cumsum(tallies), jnp.arange(rows * top), side="right").astype(jnp.int32)
    grid = labels.reshape(top, rows).T
    grid = grid[jax.random.permutation(jax.random.fold_in(own, 1), rows)]
    turn = jax.random.randint(jax.random.fold_in(own, 2), (rows, 1), 0, top)
    return jnp.take_along_axis(grid, (jnp.arange(top)[None, :] + turn) % top, axis=1)


def shares(amount, total, bound, skew, full):
    portions = [(1 << 20) // math.isqrt(grade ** skew) + 1 for grade in range(1, amount + 1)]
    largest = bound if full else min(bound, max(-(-total // amount), total * portions[0] // sum(portions)))
    least = 1 if total - largest >= amount - 1 else 0
    given, spare = [largest] + [least] * (amount - 1), total - largest - least * (amount - 1)
    while spare > 0:
        movable = [i for i in range(1, amount) if given[i] < largest] or [i for i in range(1, amount) if given[i] < bound]
        pool, left = sum([portions[i] for i in movable]), spare
        for i in movable:
            extra = min(bound - given[i], max(1, left * portions[i] // pool), spare)
            given[i] = given[i] + extra
            spare = spare - extra
    return np.array(given)


def centred(rng, extent, deviation, reach, split=(), held_as=jnp.bfloat16):
    result = deviation * jax.random.normal(rng, extent, jnp.float32)
    if split:
        result = result * level_of(rng, extent, split, -0.22, 0.18)
    return jnp.clip(result, -reach, reach).astype(held_as)


def setup_inputs(seed: int = 0) -> dict:
    key_of = jax.random.split(jax.random.key(seed), 9)
    feats = centred(key_of[0], (NODES, F), 1.0, 6.0, ((0, 32), (1, 8)))
    projection = centred(key_of[1], (F, 2 * HID), F ** -0.5, 0.1875, ((0, 8),))
    tiles = centred(key_of[2], (SLOTS, KB, BLOCK, BLOCK), (KB * BLOCK) ** -0.5, 0.25, ((0, 256),))
    slot_owner_keys = jax.random.split(jax.random.fold_in(key_of[3], 1), SLOTS // SLOTS_DEV)
    slot_owner_turns = jax.random.permutation(jax.random.fold_in(key_of[3], 3), SLOTS // SLOTS_DEV)
    slot_owner = jax.vmap(lambda own, number: assign_block(jax.random.fold_in(key_of[3], 2), own, number, SLOTS_DEV, N_DOM, 1, CAP, 2))(slot_owner_keys, slot_owner_turns).reshape((SLOTS, 1))
    slot_block = touch_ends(jax.random.randint(key_of[4], (SLOTS, 1), 0, BLK_DEV), jax.random.fold_in(key_of[4], 1), 0, BLK_DEV - 1).astype(jnp.int32)
    source_block = touch_ends(jax.random.randint(key_of[5], (SLOTS, KB), 0, BLK_DEV), jax.random.fold_in(key_of[5], 1), 0, BLK_DEV - 1).astype(jnp.int32)
    counts = touch_ends(jax.random.randint(key_of[6], (NODES,), 1, 5), jax.random.fold_in(key_of[6], 1), 1, 4).astype(jnp.int32)
    out_grad = centred(key_of[7], (NODES, HID), NODES ** -0.5, 0.015625, ((0, 256),))
    return dict(feats=feats, projection=projection, tiles=tiles, slot_owner=slot_owner, slot_block=slot_block, source_block=source_block, counts=counts, out_grad=out_grad)


def reference(feats, projection, tiles, slot_owner, slot_block, source_block, counts, out_grad):
    tile_size = tiles.shape[-1]
    out_width = out_grad.shape[1]
    devices = N_DOM * N_FEAT
    projected = jnp.dot(feats, projection, preferred_element_type=jnp.float32).astype(jnp.bfloat16)
    neighbour = projected[:, :out_width].reshape(devices, BLK_DEV, tile_size, out_width)
    self_part = projected[:, out_width:]
    tile_sets = tiles.reshape(devices, SLOTS_DEV, KB, tile_size, tile_size)
    sources = source_block.reshape(devices, SLOTS_DEV, KB)
    device_ids = jnp.arange(devices, dtype=jnp.int32)
    dest_device = slot_owner.reshape(devices, SLOTS_DEV) * N_FEAT + (device_ids % N_FEAT)[:, None]
    destination = (dest_device * BLK_DEV + slot_block.reshape(devices, SLOTS_DEV)).astype(jnp.int32)

    def accumulate(running, inputs):
        tile_set, source, blocks_here, target = inputs
        picked = blocks_here[source]
        contribution = jnp.einsum('skij,skjh->sih', tile_set.astype(jnp.float32), picked.astype(jnp.float32)).astype(jnp.bfloat16)
        return running.at[target].add(contribution.astype(jnp.float32)), None

    start_sum = jnp.zeros((devices * BLK_DEV, tile_size, out_width), jnp.float32)
    summed, unused = lax.scan(accumulate, start_sum, (tile_sets, sources, neighbour, destination))
    summed = summed.reshape(-1, out_width)
    degree = counts.astype(jnp.float32)[:, None]
    preact = summed / degree + self_part.astype(jnp.float32)
    sigma = jax.nn.sigmoid(preact)
    activated = (preact * sigma).astype(jnp.bfloat16)
    grad_pre = out_grad.astype(jnp.float32) * sigma * (1.0 + preact * (1.0 - sigma))
    grad_self = grad_pre.astype(jnp.bfloat16)
    grad_sum = (grad_pre / degree).astype(jnp.bfloat16)
    grad_blocks = grad_sum.reshape(devices * BLK_DEV, tile_size, out_width)

    def backward(inputs):
        tile_set, source, target = inputs
        slot_grad = grad_blocks[target]
        products = jnp.einsum('skij,sih->skjh', tile_set.astype(jnp.float32), slot_grad.astype(jnp.float32))
        source_hot = (jnp.arange(BLK_DEV, dtype=jnp.int32)[:, None] == source.reshape(-1)[None, :]).astype(jnp.float32)
        flat_products = products.reshape(SLOTS_DEV * KB, tile_size, out_width)
        return jnp.einsum('bn,njh->bjh', source_hot, flat_products, precision=lax.Precision.HIGHEST).astype(jnp.bfloat16)

    grad_neigh = lax.map(backward, (tile_sets, sources, destination)).reshape(-1, out_width)
    grad_proj = jnp.concatenate([grad_neigh, grad_self], axis=1)
    weight_grad = lax.dot_general(feats, grad_proj, (((0,), (0,)), ((), ())), preferred_element_type=jnp.float32)
    return activated, weight_grad
```

```python
import jax
import jax.numpy as jnp
from jax import lax
from jax.experimental import pallas as pl
from jax.experimental.pallas import tpu as pltpu
from jax.sharding import PartitionSpec as P

MESH = pl.DeviceIdType.MESH
NY, NZ, NX, NC = 4, 8, 4, 2
NF = NX * NC
BLK = 128
NB = 4
HID = 256
ROWS = NB * BLK
KB = 4
SLOTS = 32
CAP = 2
BF, F32 = jnp.bfloat16, jnp.float32


def table_kernel(owner_ref, block_ref, source_ref, idx_ref, lab_ref, src_ref, count_ref):
    def clear(p, carry):
        idx_ref[p] = 0
        lab_ref[p] = -1
        for k in range(KB):
            src_ref[p * KB + k] = 0
        return carry

    lax.fori_loop(0, NY * NZ * CAP, clear, 0)

    def clear_count(o, carry):
        count_ref[o] = 0
        return carry

    lax.fori_loop(0, NY * NZ, clear_count, 0)

    def place(s, carry):
        owner = owner_ref[s]
        seen = count_ref[owner]
        count_ref[owner] = seen + 1
        p = owner * CAP + seen
        idx_ref[p] = s
        lab_ref[p] = block_ref[s]
        for k in range(KB):
            src_ref[p * KB + k] = source_ref[s * KB + k]
        return carry

    lax.fori_loop(0, SLOTS, place, 0)


def main_kernel(
    idx, lab, src, feats, proj, tiles, out_grad, inv_deg,
    act_out, wg_out,
    fb, pb, tb, ogb, nb, selfb, ftb, ttb,
    ls, lr, cs, yr, ms, zr, sm,
    ga, bs, br, gs, gacc, prod,
    pw, rc, x1, rx, y1, ry, z1, rz, zt, zg, yt, yg,
    loc_sem, f_s, f_r, pn_s, pn_r, ps_s, ps_r, l_s, l_r,
    yf_s, yf_r, zf_s, zf_r, ag_s, ag_r, yb_s, yb_r,
    rc_s, rc_r, rx_s, rx_r, ry_s, ry_r, rz_s, rz_r, zg_s, zg_r, yg_s, yg_r,
):
    d = lax.axis_index("dom")
    f = lax.axis_index("feat")
    y, z = d // NZ, d % NZ
    x, c = f // NC, f % NC

    def to_feat(g):
        return (d, g)

    def to_yz(yy, zz):
        return (yy * NZ + zz, f)

    def remote(a, b, s, r, dev):
        return pltpu.make_async_remote_copy(
            src_ref=a, dst_ref=b, send_sem=s, recv_sem=r, device_id=dev, device_id_type=MESH
        )

    own_f = pltpu.make_async_copy(feats.at[f], fb.at[f], loc_sem.at[0])
    own_p = pltpu.make_async_copy(proj, pb.at[f], loc_sem.at[1])
    own_t = pltpu.make_async_copy(tiles, tb, loc_sem.at[2])
    own_g = pltpu.make_async_copy(out_grad, ogb, loc_sem.at[3])
    own_f.start()
    own_p.start()

    barrier = pltpu.get_barrier_semaphore()
    for o in range(1, NF):
        pl.semaphore_signal(barrier, inc=1, device_id=to_feat((f + o) % NF), device_id_type=MESH)
    for o in range(1, NY):
        pl.semaphore_signal(barrier, inc=1, device_id=to_yz((y + o) % NY, z), device_id_type=MESH)
    for o in range(1, NZ):
        pl.semaphore_signal(barrier, inc=1, device_id=to_yz(y, (z + o) % NZ), device_id_type=MESH)
    pl.semaphore_wait(barrier, NF + NY + NZ - 3)

    def f_copy(o):
        g = (f + o) % NF
        return remote(feats.at[g], fb.at[f], f_s.at[o], f_r.at[NF - o], to_feat(g))

    def p_copy(o, half, s, r):
        g = (f + o) % NF
        cols = pl.ds(half * HID, HID)
        return remote(proj.at[:, cols], pb.at[f, :, cols], s.at[o], r.at[NF - o], to_feat(g))

    for o in range(1, NF):
        f_copy(o).start()
        p_copy(o, 0, pn_s, pn_r).start()
    own_t.start()
    own_g.start()
    for o in range(1, NF):
        p_copy(o, 1, ps_s, ps_r).start()

    for o in range(NY):
        yy = (y + o) % NY

        def label_row(j, carry):
            ls[o, pl.ds(j, 1), :] = jnp.full((1, HID), lab[yy * (NZ * CAP) + j], jnp.int32)
            return carry

        lax.fori_loop(0, NZ * CAP, label_row, 0)

    def l_copy(o):
        return remote(ls.at[o], lr.at[NY - o], l_s.at[o], l_r.at[NY - o], to_yz((y + o) % NY, z))

    for o in range(1, NY):
        l_copy(o).start()
    lr[0] = ls[0]

    own_f.wait()
    own_p.wait()
    sm[...] = jnp.dot(fb[f], pb[f, :, :HID], preferred_element_type=F32)
    for o in range(1, NF):
        g = (f + o) % NF
        pltpu.make_async_copy(fb.at[g], fb.at[g], f_r.at[o]).wait()
        half = pb.at[g, :, pl.ds(0, HID)]
        pltpu.make_async_copy(half, half, pn_r.at[o]).wait()
        sm[...] += jnp.dot(fb[g], pb[g, :, :HID], preferred_element_type=F32)
    nb[...] = sm[...].astype(BF).reshape(NB, BLK, HID)
    own_t.wait()

    def far_first(t):
        return (z + NZ // 2 + (1 - 2 * (t % 2)) * ((t + 1) // 2)) % NZ

    def near_first(q):
        return (z + NZ + (1 - 2 * (q % 2)) * ((q + 1) // 2)) % NZ

    def yf_copy(t, o):
        return remote(
            cs.at[t, o], yr.at[t, NY - o], yf_s.at[t, o], yf_r.at[t, NY - o], to_yz((y + o) % NY, z)
        )

    def contribute(t, carry):
        zz = far_first(t)
        for o in range(1, NY + 1):
            r = o % NY
            yy = (y + r) % NY
            for i in range(CAP):
                p = (yy * NZ + zz) * CAP + i
                s = idx[p]
                total = None
                for k in range(0, KB, 2):
                    left = jnp.concatenate([tb[s, k], tb[s, k + 1]], axis=1)
                    right = jnp.concatenate(
                        [nb[src[p * KB + k]], nb[src[p * KB + k + 1]]], axis=0
                    )
                    part = jnp.dot(left, right, preferred_element_type=F32)
                    total = part if total is None else total + part
                if r:
                    cs[t, r, i] = total.astype(BF)
                else:
                    yr[t, 0, i] = total.astype(BF)
            if r:
                yf_copy(t, r).start()
        return carry

    lax.fori_loop(0, NZ, contribute, 0)

    sm[...] = jnp.dot(fb[f], pb[f, :, HID:], preferred_element_type=F32)
    for o in range(1, NF):
        g = (f + o) % NF
        half = pb.at[g, :, pl.ds(HID, HID)]
        pltpu.make_async_copy(half, half, ps_r.at[o]).wait()
        sm[...] += jnp.dot(fb[g], pb[g, :, HID:], preferred_element_type=F32)
    selfb[...] = sm[...].astype(BF)
    for o in range(1, NY):
        pltpu.make_async_copy(lr.at[o], lr.at[o], l_r.at[o]).wait()

    def zf_copy(t):
        return remote(ms.at[t], zr.at[t], zf_s.at[t], zf_r.at[t], to_yz(y, far_first(t)))

    def merge(t, carry):
        zz = far_first(t)
        for o in range(1, NY):
            pltpu.make_async_copy(yr.at[t, o], yr.at[t, o], yf_r.at[t, o]).wait()

        def rows(n, inner):
            part = pl.ds(pl.multiple_of(n * 32, 32), 32)
            sums = [jnp.zeros((32, HID), F32) for b in range(NB)]
            for o in range(NY):
                for i in range(CAP):
                    row = jnp.broadcast_to(lr[o, pl.ds(zz * CAP + i, 1), :], (32, HID))
                    value = yr[t, o, i, part, :].astype(F32)
                    for b in range(NB):
                        sums[b] = sums[b] + jnp.where(row == b, value, 0.0)
            for b in range(NB):
                ms[t, b, part, :] = sums[b].astype(BF)
            return inner

        lax.fori_loop(0, BLK // 32, rows, 0)

        @pl.when(t < NZ - 1)
        def _():
            zf_copy(t).start()

        def turn(n, inner):
            s = t * (SLOTS // NZ) + n
            for k in range(KB):
                ttb[s, pl.ds(k * BLK, BLK), :] = tb[s, k].T
            return inner

        lax.fori_loop(0, SLOTS // NZ, turn, 0)
        for b in range(NB):
            ftb[t, :, pl.ds(b * BLK, BLK)] = fb[t, pl.ds(b * BLK, BLK), :].T
        return carry

    lax.fori_loop(0, NZ, merge, 0)
    own_g.wait()

    def from_own(b, carry):
        rows = pl.ds(pl.multiple_of(b * BLK, BLK), BLK)
        sm[rows, :] = ms[NZ - 1, b].astype(F32)
        return carry

    lax.fori_loop(0, NB, from_own, 0)

    def gather_z(t, carry):
        pltpu.make_async_copy(zr.at[t], zr.at[t], zf_r.at[t]).wait()

        def add(b, inner):
            rows = pl.ds(pl.multiple_of(b * BLK, BLK), BLK)
            sm[rows, :] = sm[rows, :] + zr[t, b].astype(F32)
            return inner

        lax.fori_loop(0, NB, add, 0)
        return carry

    lax.fori_loop(0, NZ - 1, gather_z, 0)

    def pointwise(n, carry):
        rows = pl.ds(pl.multiple_of(n * 32, 32), 32)
        inv = inv_deg[rows, :]
        preact = sm[rows, :] * inv + selfb[rows, :].astype(F32)
        sigma = jax.nn.sigmoid(preact)
        act_out[rows, :] = (preact * sigma).astype(BF)
        grad_pre = ogb[rows, :].astype(F32) * sigma * (1.0 + preact * (1.0 - sigma))
        gs[rows, :] = grad_pre.astype(BF)
        block = n // (BLK // 32)
        ga[0, block, pl.ds(pl.multiple_of((n % (BLK // 32)) * 32, 32), 32), :] = (
            grad_pre * inv
        ).astype(BF)
        return carry

    lax.fori_loop(0, ROWS // 32, pointwise, 0)

    up, down = to_yz(y, (z + 1) % NZ), to_yz(y, (z + NZ - 1) % NZ)

    def ag_first(way):
        return remote(ga.at[0], ga.at[1 + way], ag_s.at[way], ag_r.at[way], (up, down)[way])

    def ag_next(k, way):
        q = 2 * k - 1 + way
        return remote(
            ga.at[q], ga.at[q + 2], ag_s.at[2 * k + way], ag_r.at[2 * k + way], (up, down)[way]
        )

    def ag_last(way):
        q = NZ - 3 + way
        half = pl.ds(2 * way, 2)
        return remote(
            ga.at[q, half], ga.at[NZ - 1, half], ag_s.at[6 + way], ag_r.at[6 + way], (up, down)[way]
        )

    def yb_copy(q, o):
        return remote(
            bs.at[q, o], br.at[q, NY - o], yb_s.at[q, o], yb_r.at[q, NY - o], to_yz((y + o) % NY, z)
        )

    def answer(q):
        zz = near_first(q)

        def rows(n, inner):
            part = pl.ds(pl.multiple_of(n * 32, 32), 32)
            blocks = [ga[q, b, part, :].astype(F32) for b in range(NB)]
            for o in range(NY):
                for i in range(CAP):
                    row = jnp.broadcast_to(lr[o, pl.ds(zz * CAP + i, 1), :], (32, HID))
                    value = jnp.zeros((32, HID), F32)
                    for b in range(NB):
                        value = jnp.where(row == b, blocks[b], value)
                    if o:
                        bs[q, o, i, part, :] = value.astype(BF)
                    else:
                        br[q, 0, i, part, :] = value.astype(BF)
            return inner

        lax.fori_loop(0, BLK // 32, rows, 0)
        for o in range(1, NY):
            yb_copy(q, o).start()

    def backward(q):
        zz = near_first(q)
        for o in range(1, NY):
            pltpu.make_async_copy(br.at[q, o], br.at[q, o], yb_r.at[q, o]).wait()

        def one(j, carry):
            o, i = j // CAP, j % CAP
            p = (((y + o) % NY) * NZ + zz) * CAP + i
            prod[...] = jnp.dot(ttb[idx[p]], br[q, o, i], preferred_element_type=F32)
            keep = [
                [jnp.where(src[p * KB + k] == b, 1.0, 0.0).astype(F32) for b in range(NB)]
                for k in range(KB)
            ]

            def rows(n, inner):
                base = pl.multiple_of(n * 16, 16)
                parts = [prod[pl.ds(k * BLK + base, 16), :] for k in range(KB)]
                for b in range(NB):
                    total = gacc[b, pl.ds(base, 16), :]
                    for k in range(KB):
                        total = total + keep[k][b] * parts[k]
                    gacc[b, pl.ds(base, 16), :] = total
                return inner

            lax.fori_loop(0, BLK // 16, rows, 0)
            return carry

        lax.fori_loop(0, NY * CAP, one, 0)

    def rc_copy(h):
        return remote(pw.at[h, 1 - c], rc.at[h], rc_s.at[h], rc_r.at[h], to_feat(x * NC + 1 - c))

    def rx_copy(h, o):
        xx = (x + o) % NX
        return remote(
            x1.at[h, xx], rx.at[h, NX - o], rx_s.at[h, o], rx_r.at[h, NX - o], to_feat(xx * NC + c)
        )

    def ry_copy(h, o):
        yy = (y + o) % NY
        return remote(
            y1.at[h, yy], ry.at[h, NY - o], ry_s.at[h, o], ry_r.at[h, NY - o], to_yz(yy, z)
        )

    def rz_copy(h, o):
        zz = (z + o) % NZ
        return remote(
            z1.at[h, zz], rz.at[h, NZ - o], rz_s.at[h, o], rz_r.at[h, NZ - o], to_yz(y, zz)
        )

    def zg_copy(h, o):
        zz = (z + o) % NZ
        return remote(
            zt.at[h], zg.at[h, NZ - o], zg_s.at[h, o], zg_r.at[h, NZ - o], to_yz(y, zz)
        )

    def yg_copy(h, o):
        yy = (y + o) % NY
        return remote(
            yt.at[h], yg.at[h, NY - o], yg_s.at[h, o], yg_r.at[h, NY - o], to_yz(yy, z)
        )

    def red_0(h, grad):
        for g in range(NF):
            pw[h, g % NC, g // NC] = jnp.dot(ftb[g], grad, preferred_element_type=F32)
        rc_copy(h).start()

    def red_1(h):
        rc_copy(h).wait_recv()
        for o in range(1, NX + 1):
            xx = (x + o) % NX
            x1[h, xx] = pw[h, c, xx] + rc[h, xx]
            if o < NX:
                rx_copy(h, o).start()

    def red_2(h):
        total = x1[h, x]
        for o in range(1, NX):
            pltpu.make_async_copy(rx.at[h, o], rx.at[h, o], rx_r.at[h, o]).wait()
            total = total + rx[h, o]
        y1[h] = total.reshape(NY, BLK // NY, HID)
        for o in range(1, NY):
            ry_copy(h, o).start()

    def red_3(h):
        total = y1[h, y]
        for o in range(1, NY):
            pltpu.make_async_copy(ry.at[h, o], ry.at[h, o], ry_r.at[h, o]).wait()
            total = total + ry[h, o]
        for n in range(NZ):
            r, q = n // 2, n % 2
            z1[h, n] = total[r * 8 : r * 8 + 8, q * 128 : q * 128 + 128]
        for o in range(1, NZ):
            rz_copy(h, o).start()

    def red_4(h):
        total = z1[h, z]
        for o in range(1, NZ):
            pltpu.make_async_copy(rz.at[h, o], rz.at[h, o], rz_r.at[h, o]).wait()
            total = total + rz[h, o]
        zt[h] = total
        zg[h, 0] = total
        for o in range(1, NZ):
            zg_copy(h, o).start()

    def red_5(h):
        for o in range(1, NZ):
            pltpu.make_async_copy(zg.at[h, o], zg.at[h, o], zg_r.at[h, o]).wait()
        for n in range(NZ):
            r, q = n // 2, n % 2
            yt[h, pl.ds(r * 8, 8), pl.ds(q * 128, 128)] = zg[h, (n - z + NZ) % NZ]
        for o in range(1, NY):
            yg_copy(h, o).start()

    def red_6(h):
        cols = pl.ds(HID * (1 - h), HID)
        wg_out[pl.ds(pl.multiple_of(y * (BLK // NY), BLK // NY), BLK // NY), cols] = yt[h]
        for o in range(1, NY):
            pltpu.make_async_copy(yg.at[h, o], yg.at[h, o], yg_r.at[h, o]).wait()
            rows = pl.ds(pl.multiple_of(((y + o) % NY) * (BLK // NY), BLK // NY), BLK // NY)
            wg_out[rows, cols] = yg[h, o]

    gacc[...] = jnp.zeros_like(gacc)
    ag_first(0).start()
    ag_first(1).start()
    answer(0)
    red_0(0, gs[...])
    ag_first(0).wait_recv()
    ag_first(1).wait_recv()
    ag_next(1, 0).start()
    ag_next(1, 1).start()
    answer(1)
    answer(2)
    red_1(0)
    ag_next(1, 0).wait_recv()
    ag_next(1, 1).wait_recv()
    ag_next(2, 0).start()
    ag_next(2, 1).start()
    answer(3)
    answer(4)
    red_2(0)
    backward(0)
    ag_next(2, 0).wait_recv()
    ag_next(2, 1).wait_recv()
    ag_last(0).start()
    ag_last(1).start()
    answer(5)
    answer(6)
    red_3(0)
    backward(1)
    ag_last(0).wait_recv()
    ag_last(1).wait_recv()
    answer(7)
    red_4(0)
    backward(2)
    red_5(0)
    backward(3)
    red_6(0)
    for q in range(4, NZ):
        backward(q)

    grad = gacc[...].astype(BF).reshape(ROWS, HID)
    red_0(1, grad)
    for step in (red_1, red_2, red_3, red_4, red_5, red_6):
        step(1)

    for o in range(1, NF):
        f_copy(o).wait_send()
        p_copy(o, 0, pn_s, pn_r).wait_send()
        p_copy(o, 1, ps_s, ps_r).wait_send()
    for o in range(1, NY):
        l_copy(o).wait_send()
    for t in range(NZ):
        for o in range(1, NY):
            yf_copy(t, o).wait_send()
            yb_copy(t, o).wait_send()
        if t < NZ - 1:
            zf_copy(t).wait_send()
    for way in range(2):
        ag_first(way).wait_send()
        ag_next(1, way).wait_send()
        ag_next(2, way).wait_send()
        ag_last(way).wait_send()
    for h in range(2):
        rc_copy(h).wait_send()
        for o in range(1, NX):
            rx_copy(h, o).wait_send()
        for o in range(1, NY):
            ry_copy(h, o).wait_send()
            yg_copy(h, o).wait_send()
        for o in range(1, NZ):
            rz_copy(h, o).wait_send()
            zg_copy(h, o).wait_send()


def local(feats, projection, tiles, slot_owner, slot_block, source_block, counts, out_grad):
    smem = pl.BlockSpec(memory_space=pltpu.SMEM)
    vmem = pl.BlockSpec(memory_space=pltpu.VMEM)
    hbm = pl.BlockSpec(memory_space=pl.ANY)
    places = NY * NZ * CAP
    idx, lab, src = pl.pallas_call(
        table_kernel,
        out_shape=(
            jax.ShapeDtypeStruct((places,), jnp.int32),
            jax.ShapeDtypeStruct((places,), jnp.int32),
            jax.ShapeDtypeStruct((places * KB,), jnp.int32),
        ),
        in_specs=[smem] * 3,
        out_specs=[smem] * 3,
        scratch_shapes=[pltpu.SMEM((NY * NZ,), jnp.int32)],
    )(slot_owner.reshape(-1), slot_block.reshape(-1), source_block.reshape(-1))
    inv_deg = jnp.broadcast_to((1.0 / counts.astype(F32))[:, None], (ROWS, HID))

    dma = pltpu.SemaphoreType.DMA
    scratch = [
        pltpu.VMEM((NF, ROWS, BLK), BF),
        pltpu.VMEM((NF, BLK, 2 * HID), BF),
        pltpu.VMEM((SLOTS, KB, BLK, BLK), BF),
        pltpu.VMEM((ROWS, HID), BF),
        pltpu.VMEM((NB, BLK, HID), BF),
        pltpu.VMEM((ROWS, HID), BF),
        pltpu.VMEM((NF, BLK, ROWS), BF),
        pltpu.VMEM((SLOTS, KB * BLK, BLK), BF),
        pltpu.VMEM((NY, NZ * CAP, HID), jnp.int32),
        pltpu.VMEM((NY, NZ * CAP, HID), jnp.int32),
        pltpu.VMEM((NZ, NY, CAP, BLK, HID), BF),
        pltpu.VMEM((NZ, NY, CAP, BLK, HID), BF),
        pltpu.VMEM((NZ, NB, BLK, HID), BF),
        pltpu.VMEM((NZ, NB, BLK, HID), BF),
        pltpu.VMEM((ROWS, HID), F32),
        pltpu.VMEM((NZ, NB, BLK, HID), BF),
        pltpu.VMEM((NZ, NY, CAP, BLK, HID), BF),
        pltpu.VMEM((NZ, NY, CAP, BLK, HID), BF),
        pltpu.VMEM((ROWS, HID), BF),
        pltpu.VMEM((NB, BLK, HID), F32),
        pltpu.VMEM((KB * BLK, HID), F32),
        pltpu.VMEM((2, NC, NX, BLK, HID), F32),
        pltpu.VMEM((2, NX, BLK, HID), F32),
        pltpu.VMEM((2, NX, BLK, HID), F32),
        pltpu.VMEM((2, NX, BLK, HID), F32),
        pltpu.VMEM((2, NY, BLK // NY, HID), F32),
        pltpu.VMEM((2, NY, BLK // NY, HID), F32),
        pltpu.VMEM((2, NZ, 8, 128), F32),
        pltpu.VMEM((2, NZ, 8, 128), F32),
        pltpu.VMEM((2, 8, 128), F32),
        pltpu.VMEM((2, NZ, 8, 128), F32),
        pltpu.VMEM((2, BLK // NY, HID), F32),
        pltpu.VMEM((2, NY, BLK // NY, HID), F32),
        dma((4,)),
        dma((NF,)), dma((NF,)), dma((NF,)), dma((NF,)), dma((NF,)), dma((NF,)),
        dma((NY,)), dma((NY,)),
        dma((NZ, NY)), dma((NZ, NY)), dma((NZ,)), dma((NZ,)), dma((NZ,)), dma((NZ,)),
        dma((NZ, NY)), dma((NZ, NY)),
        dma((2,)), dma((2,)), dma((2, NX)), dma((2, NX)), dma((2, NY)), dma((2, NY)),
        dma((2, NZ)), dma((2, NZ)), dma((2, NZ)), dma((2, NZ)), dma((2, NY)), dma((2, NY)),
    ]
    return pl.pallas_call(
        main_kernel,
        out_shape=(
            jax.ShapeDtypeStruct((ROWS, HID), BF),
            jax.ShapeDtypeStruct((BLK, 2 * HID), F32),
        ),
        in_specs=[smem] * 3 + [hbm] * 4 + [vmem],
        out_specs=[vmem] * 2,
        scratch_shapes=scratch,
        compiler_params=pltpu.CompilerParams(
            collective_id=0, has_side_effects=True, vmem_limit_bytes=60 << 20
        ),
    )(idx, lab, src, feats.reshape(NF, ROWS, BLK), projection, tiles, out_grad, inv_deg)


def solution(mesh):
    placed = (
        P("dom", "feat"),
        P("feat", None),
        P(("dom", "feat"), None, None, None),
        P(("dom", "feat"), None),
        P(("dom", "feat"), None),
        P(("dom", "feat"), None),
        P(("dom", "feat")),
        P(("dom", "feat"), None),
    )
    return jax.shard_map(
        local,
        mesh=mesh,
        in_specs=placed,
        out_specs=(P(("dom", "feat"), None), P("feat", None)),
        check_vma=False,
    )
```

```python
import jax
import jax.numpy as jnp
from jax import lax
from jax.experimental import pallas as pl
from jax.experimental.pallas import tpu as pltpu
from jax.sharding import PartitionSpec as P

MESH = pl.DeviceIdType.MESH
NY, NZ, NX, NC = 4, 8, 4, 2
NF = NX * NC
ND = NY * NZ
FAR_FIRST = ((2, 0), (2, 1), (1, 0), (3, 0), (1, 1), (3, 1), (0, 1))
NEAR_FIRST = FAR_FIRST[::-1]
BLK = 128
NB = 4
HID = 256
ROWS = NB * BLK
KB = 4
SLOTS = 32
CAP = 2
BF, F32 = jnp.bfloat16, jnp.float32


def main_kernel(
    owner, block, source, counts, feats, proj, tiles, out_grad,
    act_out, wg_out,
    fb, pb, tb, ogb, nb, selfb, ftb, wt, tabv, tabs, inv_deg,
    ls, lr, cs, yr, ms, zr, sm,
    ga, bs, br, gs, gacc,
    pw, rc, x1, rx, y1, ry, yt, yg,
    loc_sem, f_s, f_r, px_s, px_r, py_s, py_r, pc_s, pc_r, l_s, l_r,
    yf_s, yf_r, zf_s, zf_r, ag_s, ag_r, yb_s, yb_r,
    rc_s, rc_r, rx_s, rx_r, ry_s, ry_r, yg_s, yg_r,
):
    d = lax.axis_index("dom")
    f = lax.axis_index("feat")
    y, z = d // NZ, d % NZ
    x, c = f // NC, f % NC

    def to_feat(g):
        return (d, g)

    def to_yz(yy, zz):
        return (yy * NZ + zz, f)

    def remote(a, b, s, r, dev):
        return pltpu.make_async_remote_copy(
            src_ref=a, dst_ref=b, send_sem=s, recv_sem=r, device_id=dev, device_id_type=MESH
        )

    own_f = pltpu.make_async_copy(feats.at[f], fb.at[f], loc_sem.at[0])
    own_p = pltpu.make_async_copy(proj, pb.at[x, c], loc_sem.at[1])
    own_t = pltpu.make_async_copy(tiles, tb, loc_sem.at[2])
    own_g = pltpu.make_async_copy(out_grad, ogb, loc_sem.at[3])
    own_f.start()
    own_p.start()

    barrier = pltpu.get_barrier_semaphore()
    for o in range(1, NF):
        pl.semaphore_signal(barrier, inc=1, device_id=to_feat((f + o) % NF), device_id_type=MESH)
    for o in range(1, ND):
        pl.semaphore_signal(barrier, inc=1, device_id=((d + o) % ND, f), device_id_type=MESH)
    pl.semaphore_wait(barrier, NF + ND - 2)

    def f_copy(ox, oc):
        g = ((x + ox) % NX) * NC + (c + oc) % NC
        back = ((NX - ox) % NX) * NC + oc
        return remote(feats.at[g], fb.at[f], f_s.at[ox * NC + oc], f_r.at[back], to_feat(g))

    sibling = to_feat(x * NC + 1 - c)
    quarter = pl.ds(pl.multiple_of(y * (BLK // NY), BLK // NY), BLK // NY)

    def px_copy(o):
        return remote(
            proj.at[quarter], pb.at[x, c, quarter], px_s.at[o], px_r.at[NX - o],
            to_feat(((x + o) % NX) * NC + c),
        )

    def py_copy(o, oy):
        piece = pb.at[(x + o) % NX, c, quarter]
        return remote(
            piece, piece, py_s.at[o, oy], py_r.at[o, NY - oy], to_yz((y + oy) % NY, z)
        )

    def pc_copy(o):
        shard = pb.at[(x + o) % NX, c]
        return remote(shard if o else proj, shard, pc_s.at[o], pc_r.at[o], sibling)

    for o in (2, 1, 3):
        px_copy(o).start()
    for ox, oc in FAR_FIRST:
        f_copy(ox, oc).start()
    pc_copy(0).start()
    own_t.start()
    own_g.start()

    o_at = lax.broadcasted_iota(jnp.int32, (ND, SLOTS), 0)
    s_at = lax.broadcasted_iota(jnp.int32, (ND, SLOTS), 1)
    named = owner[...] == o_at
    before = jnp.dot(
        named.astype(BF), (o_at < s_at).astype(BF), preferred_element_type=F32
    )
    lane = lax.broadcasted_iota(jnp.int32, (ND, 128), 1)
    for i in range(CAP):
        here = named & (before == float(i))
        slot = jnp.sum(jnp.where(here, s_at.astype(F32), 0.0), axis=1, keepdims=True)
        label = jnp.sum(
            jnp.where(here, block[...].astype(F32) + 1.0, 0.0), axis=1, keepdims=True
        )
        tabv[i] = jnp.where(lane == 0, slot, 0.0).astype(jnp.int32)
        rows = jnp.broadcast_to((label - 1.0).astype(jnp.int32), (ND, HID))
        ls[:, i] = rows.reshape(NY, NZ, HID)
    picks = jnp.zeros((SLOTS, 128), F32)
    for k in range(KB):
        column = jnp.sum(
            jnp.where(o_at == s_at, source[k : k + 1, :].astype(F32), 0.0), axis=1, keepdims=True
        )
        picks = picks + jnp.where(lane == k, column, 0.0)
    tabv[CAP] = picks.astype(jnp.int32)
    table = pltpu.make_async_copy(tabv, tabs, loc_sem.at[4])
    table.start()

    def l_copy(o):
        yy = (y + o) % NY
        return remote(ls.at[yy], lr.at[NY - o], l_s.at[o], l_r.at[NY - o], to_yz(yy, z))

    for o in range(1, NY):
        l_copy(o).start()
    lr[0] = ls[y]

    for o in (1, 3, 2):
        piece = pb.at[(x + o) % NX, c, quarter]
        pltpu.make_async_copy(piece, piece, px_r.at[o]).wait()
        for oy in range(1, NY):
            py_copy(o, oy).start()

    diagonal = lax.broadcasted_iota(jnp.int32, (BLK, BLK), 0) == lax.broadcasted_iota(
        jnp.int32, (BLK, BLK), 1
    )
    for b in range(NB):
        column = jnp.sum(
            jnp.where(diagonal, counts[b : b + 1, :].astype(F32), 0.0), axis=1, keepdims=True
        )
        inv_deg[b * BLK : (b + 1) * BLK, :] = jnp.broadcast_to(1.0 / column, (BLK, HID))

    own_p.wait()
    for o in (1, 3, 2):
        for oy in range(1, NY):
            theirs = pl.ds(pl.multiple_of(((y + oy) % NY) * (BLK // NY), BLK // NY), BLK // NY)
            piece = pb.at[(x + o) % NX, c, theirs]
            pltpu.make_async_copy(piece, piece, py_r.at[o, oy]).wait()
        pc_copy(o).start()
    table.wait()

    own_f.wait()
    for o in range(NX):
        shard = pb.at[(x + o) % NX, 1 - c]
        pltpu.make_async_copy(shard, shard, pc_r.at[o]).wait()
    sm[...] = jnp.dot(fb[f], pb[x, c, :, :HID], preferred_element_type=F32)
    for ox, oc in NEAR_FIRST:
        xx, cc = (x + ox) % NX, (c + oc) % NC
        g = xx * NC + cc
        pltpu.make_async_copy(fb.at[g], fb.at[g], f_r.at[ox * NC + oc]).wait()
        sm[...] += jnp.dot(fb[g], pb[xx, cc, :, :HID], preferred_element_type=F32)
    nb[...] = sm[...].astype(BF).reshape(NB, BLK, HID)
    own_t.wait()

    def far_first(t):
        return (z + NZ // 2 + (1 - 2 * (t % 2)) * ((t + 1) // 2)) % NZ

    def near_first(q):
        return (z + NZ + (1 - 2 * (q % 2)) * ((q + 1) // 2)) % NZ

    def yf_copy(t, o):
        return remote(
            cs.at[t, o], yr.at[t, NY - o], yf_s.at[t, o], yf_r.at[t, NY - o], to_yz((y + o) % NY, z)
        )

    def slot_at(i, at):
        return jnp.clip(tabs[i, at, 0], 0, SLOTS - 1)

    def source_at(s, k):
        return jnp.clip(tabs[CAP, s, k], 0, NB - 1)

    def contribute(t, carry):
        zz = far_first(t)
        for o in range(1, NY + 1):
            r = o % NY
            yy = (y + r) % NY
            for i in range(CAP):
                s = slot_at(i, yy * NZ + zz)
                total = None
                for k in range(0, KB, 2):
                    left = jnp.concatenate([tb[s, k], tb[s, k + 1]], axis=1)
                    right = jnp.concatenate(
                        [nb[source_at(s, k)], nb[source_at(s, k + 1)]], axis=0
                    )
                    part = jnp.dot(left, right, preferred_element_type=F32)
                    total = part if total is None else total + part
                if r:
                    cs[t, r, i] = total.astype(BF)
                else:
                    yr[t, 0, i] = total.astype(BF)
            if r:
                yf_copy(t, r).start()
        return carry

    lax.fori_loop(0, NZ, contribute, 0)

    sm[...] = jnp.dot(fb[f], pb[x, c, :, HID:], preferred_element_type=F32)
    for ox, oc in NEAR_FIRST:
        xx, cc = (x + ox) % NX, (c + oc) % NC
        sm[...] += jnp.dot(fb[xx * NC + cc], pb[xx, cc, :, HID:], preferred_element_type=F32)
    selfb[...] = sm[...].astype(BF)
    for o in range(1, NY):
        pltpu.make_async_copy(lr.at[o], lr.at[o], l_r.at[o]).wait()

    def zf_copy(t):
        return remote(ms.at[t], zr.at[t], zf_s.at[t], zf_r.at[t], to_yz(y, far_first(t)))

    def merge(t, carry):
        zz = far_first(t)
        for o in range(1, NY):
            pltpu.make_async_copy(yr.at[t, o], yr.at[t, o], yf_r.at[t, o]).wait()

        def rows(n, inner):
            part = pl.ds(pl.multiple_of(n * 32, 32), 32)
            sums = [jnp.zeros((32, HID), F32) for b in range(NB)]
            for o in range(NY):
                for i in range(CAP):
                    row = jnp.broadcast_to(lr[o, i, pl.ds(zz, 1), :], (32, HID))
                    value = yr[t, o, i, part, :].astype(F32)
                    for b in range(NB):
                        sums[b] = sums[b] + jnp.where(row == b, value, 0.0)
            for b in range(NB):
                ms[t, b, part, :] = sums[b].astype(BF)
            return inner

        lax.fori_loop(0, BLK // 32, rows, 0)

        @pl.when(t < NZ - 1)
        def _():
            zf_copy(t).start()

        def turn(n, inner):
            s = t * (SLOTS // NZ) + n
            parts = [tb[s, k].astype(F32) for k in range(KB)]
            for b in range(NB):
                total = jnp.zeros((BLK, BLK), F32)
                for k in range(KB):
                    total = total + jnp.where(source_at(s, k) == b, parts[k], 0.0)
                wt[s, pl.ds(b * BLK, BLK), :] = total.astype(BF).T
            return inner

        lax.fori_loop(0, SLOTS // NZ, turn, 0)
        for b in range(NB):
            ftb[t, :, pl.ds(b * BLK, BLK)] = fb[t, pl.ds(b * BLK, BLK), :].T
        return carry

    lax.fori_loop(0, NZ, merge, 0)
    own_g.wait()

    def from_own(b, carry):
        rows = pl.ds(pl.multiple_of(b * BLK, BLK), BLK)
        sm[rows, :] = ms[NZ - 1, b].astype(F32)
        return carry

    lax.fori_loop(0, NB, from_own, 0)

    def gather_z(t, carry):
        pltpu.make_async_copy(zr.at[t], zr.at[t], zf_r.at[t]).wait()

        def add(b, inner):
            rows = pl.ds(pl.multiple_of(b * BLK, BLK), BLK)
            sm[rows, :] = sm[rows, :] + zr[t, b].astype(F32)
            return inner

        lax.fori_loop(0, NB, add, 0)
        return carry

    lax.fori_loop(0, NZ - 1, gather_z, 0)

    def pointwise(n, carry):
        rows = pl.ds(pl.multiple_of(n * 32, 32), 32)
        inv = inv_deg[rows, :]
        preact = sm[rows, :] * inv + selfb[rows, :].astype(F32)
        sigma = jax.nn.sigmoid(preact)
        act_out[rows, :] = (preact * sigma).astype(BF)
        grad_pre = ogb[rows, :].astype(F32) * sigma * (1.0 + preact * (1.0 - sigma))
        gs[rows, :] = grad_pre.astype(BF)
        block = n // (BLK // 32)
        ga[0, block, pl.ds(pl.multiple_of((n % (BLK // 32)) * 32, 32), 32), :] = (
            grad_pre * inv
        ).astype(BF)
        return carry

    lax.fori_loop(0, ROWS // 32, pointwise, 0)

    up, down = to_yz(y, (z + 1) % NZ), to_yz(y, (z + NZ - 1) % NZ)

    def ag_first(way):
        return remote(ga.at[0], ga.at[1 + way], ag_s.at[way], ag_r.at[way], (up, down)[way])

    def ag_next(k, way):
        q = 2 * k - 1 + way
        return remote(
            ga.at[q], ga.at[q + 2], ag_s.at[2 * k + way], ag_r.at[2 * k + way], (up, down)[way]
        )

    def ag_last(way):
        q = NZ - 3 + way
        half = pl.ds(2 * way, 2)
        return remote(
            ga.at[q, half], ga.at[NZ - 1, half], ag_s.at[6 + way], ag_r.at[6 + way], (up, down)[way]
        )

    def yb_copy(q, o):
        return remote(
            bs.at[q, o], br.at[q, NY - o], yb_s.at[q, o], yb_r.at[q, NY - o], to_yz((y + o) % NY, z)
        )

    def answer(q):
        zz = near_first(q)

        def rows(n, inner):
            part = pl.ds(pl.multiple_of(n * 32, 32), 32)
            blocks = [ga[q, b, part, :].astype(F32) for b in range(NB)]
            for o in range(NY):
                for i in range(CAP):
                    row = jnp.broadcast_to(lr[o, i, pl.ds(zz, 1), :], (32, HID))
                    value = jnp.zeros((32, HID), F32)
                    for b in range(NB):
                        value = jnp.where(row == b, blocks[b], value)
                    if o:
                        bs[q, o, i, part, :] = value.astype(BF)
                    else:
                        br[q, 0, i, part, :] = value.astype(BF)
            return inner

        lax.fori_loop(0, BLK // 32, rows, 0)
        for o in range(1, NY):
            yb_copy(q, o).start()

    def backward(q):
        zz = near_first(q)
        for o in range(1, NY):
            pltpu.make_async_copy(br.at[q, o], br.at[q, o], yb_r.at[q, o]).wait()

        def pair(r, carry):
            at = ((y + r) % NY) * NZ + zz
            left = jnp.concatenate([wt[slot_at(0, at)], wt[slot_at(1, at)]], axis=1)
            right = br[q, r].reshape(CAP * BLK, HID)
            gacc[...] += jnp.dot(left, right, preferred_element_type=F32)
            return carry

        lax.fori_loop(0, NY, pair, 0)

    def rc_copy(h, o):
        xx = (x + o) % NX
        return remote(pw.at[h, xx], rc.at[h, xx], rc_s.at[h, o], rc_r.at[h, o], sibling)

    def rx_copy(h, o):
        xx = (x + o) % NX
        return remote(
            x1.at[h, xx], rx.at[h, NX - o], rx_s.at[h, o], rx_r.at[h, NX - o], to_feat(xx * NC + c)
        )

    def ry_copy(h, o):
        e = (d + o) % ND
        return remote(y1.at[h, e], ry.at[h, ND - o], ry_s.at[h], ry_r.at[h], (e, f))

    def yg_copy(h, o):
        return remote(yt.at[h], yg.at[h, ND - o], yg_s.at[h], yg_r.at[h], ((d + o) % ND, f))

    def red_0(h, grad):
        for o in (2, 1, 3, 0):
            xx = (x + o) % NX
            pw[h, xx] = jnp.dot(ftb[xx * NC + 1 - c], grad, preferred_element_type=F32)
            rc_copy(h, o).start()
        for o in (2, 1, 3, 0):
            xx = (x + o) % NX
            x1[h, xx] = jnp.dot(ftb[xx * NC + c], grad, preferred_element_type=F32)

    def red_1(h):
        for o in (2, 1, 3, 0):
            xx = (x + o) % NX
            rc_copy(h, o).wait_recv()
            x1[h, xx] = x1[h, xx] + rc[h, xx]
            if o:
                rx_copy(h, o).start()

    def red_2(h):
        total = x1[h, x]
        for o in (1, 3, 2):
            pltpu.make_async_copy(rx.at[h, o], rx.at[h, o], rx_r.at[h, o]).wait()
            total = total + rx[h, o]
        for n in range(ND):
            r, q = n // 2, n % 2
            y1[h, n] = total[r * 8 : r * 8 + 8, q * 128 : q * 128 + 128]

        def send(o, carry):
            ry_copy(h, o).start()
            return carry

        lax.fori_loop(1, ND, send, 0)

    def others(buf, h):
        return buf.at[h, pl.ds(1, ND - 1)]

    def red_3(h):
        total = y1[h, d]
        pltpu.make_async_copy(others(ry, h), others(ry, h), ry_r.at[h]).wait()
        for o in range(1, ND):
            total = total + ry[h, o]
        yt[h] = total
        yg[h, 0] = total

        def send(o, carry):
            yg_copy(h, o).start()
            return carry

        lax.fori_loop(1, ND, send, 0)

    def red_4(h):
        pltpu.make_async_copy(others(yg, h), others(yg, h), yg_r.at[h]).wait()
        for n in range(ND):
            r, q = n // 2, n % 2
            wg_out[pl.ds(r * 8, 8), pl.ds(HID * (1 - h) + q * 128, 128)] = yg[h, (n - d + ND) % ND]

    gacc[...] = jnp.zeros_like(gacc)
    ag_first(0).start()
    ag_first(1).start()
    answer(0)
    red_0(0, gs[...])
    ag_first(0).wait_recv()
    ag_first(1).wait_recv()
    ag_next(1, 0).start()
    ag_next(1, 1).start()
    answer(1)
    answer(2)
    red_1(0)
    ag_next(1, 0).wait_recv()
    ag_next(1, 1).wait_recv()
    ag_next(2, 0).start()
    ag_next(2, 1).start()
    answer(3)
    answer(4)
    red_2(0)
    backward(0)
    ag_next(2, 0).wait_recv()
    ag_next(2, 1).wait_recv()
    ag_last(0).start()
    ag_last(1).start()
    answer(5)
    answer(6)
    red_3(0)
    backward(1)
    ag_last(0).wait_recv()
    ag_last(1).wait_recv()
    answer(7)
    red_4(0)
    backward(2)
    backward(3)
    for q in range(4, NZ):
        backward(q)

    grad = gacc[...].astype(BF)
    red_0(1, grad)
    for step in (red_1, red_2, red_3, red_4):
        step(1)

    for ox, oc in FAR_FIRST:
        f_copy(ox, oc).wait_send()
    for o in range(1, NX):
        px_copy(o).wait_send()
        for oy in range(1, NY):
            py_copy(o, oy).wait_send()
    for o in range(NX):
        pc_copy(o).wait_send()
    for o in range(1, NY):
        l_copy(o).wait_send()
    for t in range(NZ):
        for o in range(1, NY):
            yf_copy(t, o).wait_send()
            yb_copy(t, o).wait_send()
        if t < NZ - 1:
            zf_copy(t).wait_send()
    for way in range(2):
        ag_first(way).wait_send()
        ag_next(1, way).wait_send()
        ag_next(2, way).wait_send()
        ag_last(way).wait_send()
    for h in range(2):
        for o in range(NX):
            rc_copy(h, o).wait_send()
        for o in range(1, NX):
            rx_copy(h, o).wait_send()
        for buf, sem in ((ry, ry_s), (yg, yg_s)):
            pltpu.make_async_copy(others(buf, h), others(buf, h), sem.at[h]).wait()


def local(feats, projection, tiles, slot_owner, slot_block, source_block, counts, out_grad):
    vmem = pl.BlockSpec(memory_space=pltpu.VMEM)
    hbm = pl.BlockSpec(memory_space=pl.ANY)
    dma = pltpu.SemaphoreType.DMA
    scratch = [
        pltpu.VMEM((NF, ROWS, BLK), BF),
        pltpu.VMEM((NX, NC, BLK, 2 * HID), BF),
        pltpu.VMEM((SLOTS, KB, BLK, BLK), BF),
        pltpu.VMEM((ROWS, HID), BF),
        pltpu.VMEM((NB, BLK, HID), BF),
        pltpu.VMEM((ROWS, HID), BF),
        pltpu.VMEM((NF, BLK, ROWS), BF),
        pltpu.VMEM((SLOTS, NB * BLK, BLK), BF),
        pltpu.VMEM((CAP + 1, ND, 128), jnp.int32),
        pltpu.SMEM((CAP + 1, ND, 128), jnp.int32),
        pltpu.VMEM((ROWS, HID), F32),
        pltpu.VMEM((NY, CAP, NZ, HID), jnp.int32),
        pltpu.VMEM((NY, CAP, NZ, HID), jnp.int32),
        pltpu.VMEM((NZ, NY, CAP, BLK, HID), BF),
        pltpu.VMEM((NZ, NY, CAP, BLK, HID), BF),
        pltpu.VMEM((NZ, NB, BLK, HID), BF),
        pltpu.VMEM((NZ, NB, BLK, HID), BF),
        pltpu.VMEM((ROWS, HID), F32),
        pltpu.VMEM((NZ, NB, BLK, HID), BF),
        pltpu.VMEM((NZ, NY, CAP, BLK, HID), BF),
        pltpu.VMEM((NZ, NY, CAP, BLK, HID), BF),
        pltpu.VMEM((ROWS, HID), BF),
        pltpu.VMEM((ROWS, HID), F32),
        pltpu.VMEM((2, NX, BLK, HID), F32),
        pltpu.VMEM((2, NX, BLK, HID), F32),
        pltpu.VMEM((2, NX, BLK, HID), F32),
        pltpu.VMEM((2, NX, BLK, HID), F32),
        pltpu.VMEM((2, ND, 8, 128), F32),
        pltpu.VMEM((2, ND, 8, 128), F32),
        pltpu.VMEM((2, 8, 128), F32),
        pltpu.VMEM((2, ND, 8, 128), F32),
        dma((5,)),
        dma((NF,)), dma((NF,)), dma((NX,)), dma((NX,)), dma((NX, NY)), dma((NX, NY)),
        dma((NX,)), dma((NX,)), dma((NY,)), dma((NY,)),
        dma((NZ, NY)), dma((NZ, NY)), dma((NZ,)), dma((NZ,)), dma((NZ,)), dma((NZ,)),
        dma((NZ, NY)), dma((NZ, NY)),
        dma((2, NX)), dma((2, NX)), dma((2, NX)), dma((2, NX)),
        dma((2,)), dma((2,)), dma((2,)), dma((2,)),
    ]
    return pl.pallas_call(
        main_kernel,
        out_shape=(
            jax.ShapeDtypeStruct((ROWS, HID), BF),
            jax.ShapeDtypeStruct((BLK, 2 * HID), F32),
        ),
        in_specs=[vmem] * 4 + [hbm] * 4,
        out_specs=[vmem] * 2,
        scratch_shapes=scratch,
        compiler_params=pltpu.CompilerParams(
            collective_id=0, has_side_effects=True, vmem_limit_bytes=60 << 20
        ),
    )(
        slot_owner.reshape(1, SLOTS),
        slot_block.reshape(1, SLOTS),
        source_block.T,
        counts.reshape(NB, BLK),
        feats.reshape(NF, ROWS, BLK),
        projection,
        tiles,
        out_grad,
    )


def solution(mesh):
    placed = (
        P("dom", "feat"),
        P("feat", None),
        P(("dom", "feat"), None, None, None),
        P(("dom", "feat"), None),
        P(("dom", "feat"), None),
        P(("dom", "feat"), None),
        P(("dom", "feat")),
        P(("dom", "feat"), None),
    )
    return jax.shard_map(
        local,
        mesh=mesh,
        in_specs=placed,
        out_specs=(P(("dom", "feat"), None), P("feat", None)),
        check_vma=False,
    )
```

```python
import jax
import jax.numpy as jnp
from jax import lax
from jax.experimental import pallas as pl
from jax.experimental.pallas import tpu as pltpu
from jax.sharding import PartitionSpec as P

MESH = pl.DeviceIdType.MESH
NY, NZ, NX, NC = 4, 8, 4, 2
NF = NX * NC
ND = NY * NZ
FAR_FIRST = ((2, 0), (2, 1), (1, 0), (3, 0), (1, 1), (3, 1), (0, 1))
NEAR_FIRST = FAR_FIRST[::-1]
BLK = 128
HALF = 64
NB = 4
HID = 256
ROWS = NB * BLK
KB = 4
SLOTS = 32
CAP = 2
BF, F32 = jnp.bfloat16, jnp.float32


def main_kernel(
    owner, block, source, counts, feats, proj, tiles, out_grad,
    act_out, wg_out,
    fb, pb, tb, ogb, nb, selfb, ftb, wt, tabv, tabs, inv_deg,
    ls, lr, cs, yr, ms, zr, zx, zy, sm,
    ga, bs, br, gs, gacc,
    pw, rc, x1, rx, y1, ry, yt, yg,
    loc_sem, f_s, f_r, px_s, px_r, py_s, py_r, pc_s, pc_r, l_s, l_r,
    yf_s, yf_r, zf_s, zf_r, zx_s, zx_r, zy_s, zy_r, ag_s, ag_r, yb_s, yb_r,
    rc_s, rc_r, rx_s, rx_r, ry_s, ry_r, yg_s, yg_r,
):
    d = lax.axis_index("dom")
    f = lax.axis_index("feat")
    y, z = d // NZ, d % NZ
    x, c = f // NC, f % NC

    def to_feat(g):
        return (d, g)

    def to_yz(yy, zz):
        return (yy * NZ + zz, f)

    def remote(a, b, s, r, dev):
        return pltpu.make_async_remote_copy(
            src_ref=a, dst_ref=b, send_sem=s, recv_sem=r, device_id=dev, device_id_type=MESH
        )

    own_f = pltpu.make_async_copy(feats.at[f], fb.at[f], loc_sem.at[0])
    own_p = pltpu.make_async_copy(proj, pb.at[x, c], loc_sem.at[1])
    own_t = pltpu.make_async_copy(tiles, tb, loc_sem.at[2])
    own_g = pltpu.make_async_copy(out_grad, ogb, loc_sem.at[3])
    own_f.start()
    own_p.start()

    barrier = pltpu.get_barrier_semaphore()
    for o in range(1, NF):
        pl.semaphore_signal(barrier, inc=1, device_id=to_feat((f + o) % NF), device_id_type=MESH)
    for o in range(1, ND):
        pl.semaphore_signal(barrier, inc=1, device_id=((d + o) % ND, f), device_id_type=MESH)
    pl.semaphore_wait(barrier, NF + ND - 2)

    def f_copy(ox, oc):
        g = ((x + ox) % NX) * NC + (c + oc) % NC
        back = ((NX - ox) % NX) * NC + oc
        return remote(feats.at[g], fb.at[f], f_s.at[ox * NC + oc], f_r.at[back], to_feat(g))

    sibling = to_feat(x * NC + 1 - c)
    quarter = pl.ds(pl.multiple_of(y * (BLK // NY), BLK // NY), BLK // NY)

    def px_copy(o):
        return remote(
            proj.at[quarter], pb.at[x, c, quarter], px_s.at[o], px_r.at[NX - o],
            to_feat(((x + o) % NX) * NC + c),
        )

    def py_copy(o, oy):
        piece = pb.at[(x + o) % NX, c, quarter]
        return remote(
            piece, piece, py_s.at[o, oy], py_r.at[o, NY - oy], to_yz((y + oy) % NY, z)
        )

    def pc_copy(o):
        shard = pb.at[(x + o) % NX, c]
        return remote(shard if o else proj, shard, pc_s.at[o], pc_r.at[o], sibling)

    for o in (2, 1, 3):
        px_copy(o).start()
    for ox, oc in FAR_FIRST:
        f_copy(ox, oc).start()
    pc_copy(0).start()
    own_t.start()
    own_g.start()

    o_at = lax.broadcasted_iota(jnp.int32, (ND, SLOTS), 0)
    s_at = lax.broadcasted_iota(jnp.int32, (ND, SLOTS), 1)
    named = owner[...] == o_at
    before = jnp.dot(
        named.astype(BF), (o_at < s_at).astype(BF), preferred_element_type=F32
    )
    lane = lax.broadcasted_iota(jnp.int32, (ND, 128), 1)
    for i in range(CAP):
        here = named & (before == float(i))
        slot = jnp.sum(jnp.where(here, s_at.astype(F32), 0.0), axis=1, keepdims=True)
        label = jnp.sum(
            jnp.where(here, block[...].astype(F32) + 1.0, 0.0), axis=1, keepdims=True
        )
        tabv[i] = jnp.where(lane == 0, slot, 0.0).astype(jnp.int32)
        rows = jnp.broadcast_to((label - 1.0).astype(jnp.int32), (ND, HID))
        ls[:, i] = rows.reshape(NY, NZ, HID)
    picks = jnp.zeros((SLOTS, 128), F32)
    for k in range(KB):
        column = jnp.sum(
            jnp.where(o_at == s_at, source[k : k + 1, :].astype(F32), 0.0), axis=1, keepdims=True
        )
        picks = picks + jnp.where(lane == k, column, 0.0)
    tabv[CAP] = picks.astype(jnp.int32)
    table = pltpu.make_async_copy(tabv, tabs, loc_sem.at[4])
    table.start()

    def l_copy(o):
        yy = (y + o) % NY
        return remote(ls.at[yy], lr.at[NY - o], l_s.at[o], l_r.at[NY - o], to_yz(yy, z))

    for o in range(1, NY):
        l_copy(o).start()
    lr[0] = ls[y]

    for o in (1, 3, 2):
        piece = pb.at[(x + o) % NX, c, quarter]
        pltpu.make_async_copy(piece, piece, px_r.at[o]).wait()
        for oy in range(1, NY):
            py_copy(o, oy).start()

    diagonal = lax.broadcasted_iota(jnp.int32, (BLK, BLK), 0) == lax.broadcasted_iota(
        jnp.int32, (BLK, BLK), 1
    )
    for b in range(NB):
        column = jnp.sum(
            jnp.where(diagonal, counts[b : b + 1, :].astype(F32), 0.0), axis=1, keepdims=True
        )
        inv_deg[b * BLK : (b + 1) * BLK, :] = jnp.broadcast_to(1.0 / column, (BLK, HID))

    own_p.wait()
    for o in (1, 3, 2):
        for oy in range(1, NY):
            theirs = pl.ds(pl.multiple_of(((y + oy) % NY) * (BLK // NY), BLK // NY), BLK // NY)
            piece = pb.at[(x + o) % NX, c, theirs]
            pltpu.make_async_copy(piece, piece, py_r.at[o, oy]).wait()
        pc_copy(o).start()
    table.wait()

    own_f.wait()
    for o in range(NX):
        shard = pb.at[(x + o) % NX, 1 - c]
        pltpu.make_async_copy(shard, shard, pc_r.at[o]).wait()
    sm[...] = jnp.dot(fb[f], pb[x, c, :, :HID], preferred_element_type=F32)
    for ox, oc in NEAR_FIRST:
        xx, cc = (x + ox) % NX, (c + oc) % NC
        g = xx * NC + cc
        pltpu.make_async_copy(fb.at[g], fb.at[g], f_r.at[ox * NC + oc]).wait()
        sm[...] += jnp.dot(fb[g], pb[xx, cc, :, :HID], preferred_element_type=F32)
    nb[...] = sm[...].astype(BF).reshape(NB, BLK, HID)
    own_t.wait()

    def far_first(t):
        return (z + NZ // 2 + (1 - 2 * (t % 2)) * ((t + 1) // 2)) % NZ

    def near_first(q):
        return (z + NZ + (1 - 2 * (q % 2)) * ((q + 1) // 2)) % NZ

    def yf_copy(t, o):
        return remote(
            cs.at[t, o], yr.at[t, NY - o], yf_s.at[t, o], yf_r.at[t, NY - o], to_yz((y + o) % NY, z)
        )

    def slot_at(i, at):
        return jnp.clip(tabs[i, at, 0], 0, SLOTS - 1)

    def source_at(s, k):
        return jnp.clip(tabs[CAP, s, k], 0, NB - 1)

    def contribute(t, carry):
        zz = far_first(t)
        for o in range(1, NY + 1):
            r = o % NY
            yy = (y + r) % NY
            for i in range(CAP):
                s = slot_at(i, yy * NZ + zz)
                total = None
                for k in range(0, KB, 2):
                    left = jnp.concatenate([tb[s, k], tb[s, k + 1]], axis=1)
                    right = jnp.concatenate(
                        [nb[source_at(s, k)], nb[source_at(s, k + 1)]], axis=0
                    )
                    part = jnp.dot(left, right, preferred_element_type=F32)
                    total = part if total is None else total + part
                if r:
                    cs[t, r, i] = total.astype(BF)
                else:
                    yr[t, 0, i] = total.astype(BF)
            if r:
                yf_copy(t, r).start()
        return carry

    lax.fori_loop(0, NZ, contribute, 0)

    sm[...] = jnp.dot(fb[f], pb[x, c, :, HID:], preferred_element_type=F32)
    for ox, oc in NEAR_FIRST:
        xx, cc = (x + ox) % NX, (c + oc) % NC
        sm[...] += jnp.dot(fb[xx * NC + cc], pb[xx, cc, :, HID:], preferred_element_type=F32)
    selfb[...] = sm[...].astype(BF)
    for o in range(1, NY):
        pltpu.make_async_copy(lr.at[o], lr.at[o], l_r.at[o]).wait()

    def along_z(o):
        return to_yz(y, (z + o + NZ) % NZ)

    def zf_copy(t):
        return remote(ms.at[t], zr.at[t], zf_s.at[t], zf_r.at[t], along_z({3: 2, 4: -2, 5: 1, 6: -1}[t]))

    def zx_copy(way):
        half = ms.at[0, pl.ds(2 * way, 2)]
        return remote(half, zx.at[way], zx_s.at[way], zx_r.at[way], along_z((2, -2)[way]))

    def zy_copy(way):
        return remote(ms.at[1 + way], zy.at[way], zy_s.at[way], zy_r.at[way], along_z((1, -1)[way]))

    def merge(t):
        zz = far_first(t)
        for o in range(1, NY):
            pltpu.make_async_copy(yr.at[t, o], yr.at[t, o], yf_r.at[t, o]).wait()
        way = t - 3
        if way in (0, 1):
            zx_copy(way).wait_recv()
            zy_copy(way).wait_recv()

        def rows(n, inner):
            part = pl.ds(pl.multiple_of(n * 32, 32), 32)
            sums = [jnp.zeros((32, HID), F32) for b in range(NB)]
            for o in range(NY):
                for i in range(CAP):
                    row = jnp.broadcast_to(lr[o, i, pl.ds(zz, 1), :], (32, HID))
                    value = yr[t, o, i, part, :].astype(F32)
                    for b in range(NB):
                        sums[b] = sums[b] + jnp.where(row == b, value, 0.0)
            for b in range(NB):
                if way in (0, 1):
                    sums[b] = sums[b] + zy[way, b, part, :].astype(F32)
                    if b // 2 == way:
                        sums[b] = sums[b] + zx[way, b % 2, part, :].astype(F32)
                if t < NZ - 1:
                    ms[t, b, part, :] = sums[b].astype(BF)
                else:
                    sm[pl.ds(pl.multiple_of(b * BLK + n * 32, 32), 32), :] = sums[b]
            return inner

        lax.fori_loop(0, BLK // 32, rows, 0)
        if t == 0:
            zx_copy(0).start()
            zx_copy(1).start()
        elif t < 3:
            zy_copy(t - 1).start()
        elif t < NZ - 1:
            zf_copy(t).start()

        def turn(n, inner):
            s = t * (SLOTS // (NZ - 1)) + n
            parts = [tb[s, k].astype(F32) for k in range(KB)]
            for b in range(NB):
                total = jnp.zeros((BLK, BLK), F32)
                for k in range(KB):
                    total = total + jnp.where(source_at(s, k) == b, parts[k], 0.0)
                wt[s, pl.ds(b * BLK, BLK), :] = total.astype(BF).T
            return inner

        if t < NZ - 1:
            most = SLOTS // (NZ - 1)
            lax.fori_loop(0, most if t < NZ - 2 else SLOTS - t * most, turn, 0)
            for g in (t, NZ - 1) if t == NZ - 2 else (t,):
                for b in range(NB):
                    ftb[g, :, pl.ds(b * BLK, BLK)] = fb[g, pl.ds(b * BLK, BLK), :].T

    for t in range(NZ):
        merge(t)
    own_g.wait()

    for t in range(3, NZ - 1):
        pltpu.make_async_copy(zr.at[t], zr.at[t], zf_r.at[t]).wait()

        def add(b, inner):
            rows = pl.ds(pl.multiple_of(b * BLK, BLK), BLK)
            sm[rows, :] = sm[rows, :] + zr[t, b].astype(F32)
            return inner

        lax.fori_loop(0, NB, add, 0)

    def pointwise(u):
        def some(n, carry):
            b, m = n // 2, n % 2
            rows = pl.ds(pl.multiple_of(b * BLK + u * HALF + m * 32, 32), 32)
            inv = inv_deg[rows, :]
            preact = sm[rows, :] * inv + selfb[rows, :].astype(F32)
            sigma = jax.nn.sigmoid(preact)
            act_out[rows, :] = (preact * sigma).astype(BF)
            grad_pre = ogb[rows, :].astype(F32) * sigma * (1.0 + preact * (1.0 - sigma))
            gs[rows, :] = grad_pre.astype(BF)
            ga[0, b, u, pl.ds(pl.multiple_of(m * 32, 32), 32), :] = (grad_pre * inv).astype(BF)
            return carry

        lax.fori_loop(0, NB * 2, some, 0)

    up, down = to_yz(y, (z + 1) % NZ), to_yz(y, (z + NZ - 1) % NZ)

    def ag_copy(k, way, u):
        q = 2 * k - 1 + way if k else 0
        blocks = pl.ds(0, NB) if k < NZ // 2 - 1 else pl.ds(2 * way, 2)
        to = 2 * k + 1 + way if k < NZ // 2 - 1 else NZ - 1
        return remote(
            ga.at[q, blocks, u], ga.at[to, blocks, u],
            ag_s.at[2 * k + way, u], ag_r.at[2 * k + way, u], (up, down)[way],
        )

    def yb_copy(q, o, u):
        return remote(
            bs.at[q, o, :, u], br.at[q, NY - o, :, u], yb_s.at[q, o, u], yb_r.at[q, NY - o, u],
            to_yz((y + o) % NY, z),
        )

    def answer(q, u):
        zz = near_first(q)

        def rows(n, inner):
            part = pl.ds(pl.multiple_of(n * 32, 32), 32)
            blocks = [ga[q, b, u, part, :].astype(F32) for b in range(NB)]
            for o in range(NY):
                for i in range(CAP):
                    row = jnp.broadcast_to(lr[o, i, pl.ds(zz, 1), :], (32, HID))
                    value = jnp.zeros((32, HID), F32)
                    for b in range(NB):
                        value = jnp.where(row == b, blocks[b], value)
                    if o:
                        bs[q, o, i, u, part, :] = value.astype(BF)
                    else:
                        br[q, 0, i, u, part, :] = value.astype(BF)
            return inner

        lax.fori_loop(0, HALF // 32, rows, 0)
        for o in range(1, NY):
            yb_copy(q, o, u).start()

    def backward(q):
        zz = near_first(q)
        for o in range(1, NY):
            for u in range(2):
                piece = br.at[q, o, :, u]
                pltpu.make_async_copy(piece, piece, yb_r.at[q, o, u]).wait()

        def pair(r, carry):
            at = ((y + r) % NY) * NZ + zz
            left = jnp.concatenate([wt[slot_at(0, at)], wt[slot_at(1, at)]], axis=1)
            right = br[q, r].reshape(CAP * BLK, HID)
            gacc[...] += jnp.dot(left, right, preferred_element_type=F32)
            return carry

        lax.fori_loop(0, NY, pair, 0)

    def rc_copy(h, o):
        xx = (x + o) % NX
        return remote(pw.at[h, xx], rc.at[h, xx], rc_s.at[h, o], rc_r.at[h, o], sibling)

    def rx_copy(h, o):
        xx = (x + o) % NX
        return remote(
            x1.at[h, xx], rx.at[h, NX - o], rx_s.at[h, o], rx_r.at[h, NX - o], to_feat(xx * NC + c)
        )

    def ry_copy(h, o):
        e = (d + o) % ND
        return remote(y1.at[h, e], ry.at[h, ND - o], ry_s.at[h], ry_r.at[h], (e, f))

    def yg_copy(h, o):
        return remote(yt.at[h], yg.at[h, ND - o], yg_s.at[h], yg_r.at[h], ((d + o) % ND, f))

    def red_0(h, grad):
        for o in (2, 1, 3, 0):
            xx = (x + o) % NX
            pw[h, xx] = jnp.dot(ftb[xx * NC + 1 - c], grad, preferred_element_type=F32)
            rc_copy(h, o).start()
        for o in (2, 1, 3, 0):
            xx = (x + o) % NX
            x1[h, xx] = jnp.dot(ftb[xx * NC + c], grad, preferred_element_type=F32)

    def red_1(h):
        for o in (2, 1, 3, 0):
            xx = (x + o) % NX
            rc_copy(h, o).wait_recv()
            x1[h, xx] = x1[h, xx] + rc[h, xx]
            if o:
                rx_copy(h, o).start()

    def red_2(h):
        total = x1[h, x]
        for o in (1, 3, 2):
            pltpu.make_async_copy(rx.at[h, o], rx.at[h, o], rx_r.at[h, o]).wait()
            total = total + rx[h, o]
        for n in range(ND):
            r, q = n // 2, n % 2
            y1[h, n] = total[r * 8 : r * 8 + 8, q * 128 : q * 128 + 128]

        def send(o, carry):
            ry_copy(h, o).start()
            return carry

        lax.fori_loop(1, ND, send, 0)

    def others(buf, h):
        return buf.at[h, pl.ds(1, ND - 1)]

    def red_3(h):
        total = y1[h, d]
        pltpu.make_async_copy(others(ry, h), others(ry, h), ry_r.at[h]).wait()
        for o in range(1, ND):
            total = total + ry[h, o]
        yt[h] = total
        yg[h, 0] = total

        def send(o, carry):
            yg_copy(h, o).start()
            return carry

        lax.fori_loop(1, ND, send, 0)

    def red_4(h):
        pltpu.make_async_copy(others(yg, h), others(yg, h), yg_r.at[h]).wait()
        for n in range(ND):
            r, q = n // 2, n % 2
            wg_out[pl.ds(r * 8, 8), pl.ds(HID * (1 - h) + q * 128, 128)] = yg[h, (n - d + ND) % ND]

    gacc[...] = jnp.zeros_like(gacc)
    for u in range(2):
        pointwise(u)
        for way in range(2):
            ag_copy(0, way, u).start()
        answer(0, u)

    def pass_on(k):
        for u in range(2):
            for way in range(2):
                ag_copy(k - 1, way, u).wait_recv()
                if k < NZ // 2:
                    ag_copy(k, way, u).start()
            if k < NZ // 2:
                answer(2 * k - 1, u)
                answer(2 * k, u)
            else:
                answer(NZ - 1, u)

    red_0(0, gs[...])
    pass_on(1)
    red_1(0)
    backward(0)
    pass_on(2)
    red_2(0)
    backward(1)
    pass_on(3)
    red_3(0)
    backward(2)
    pass_on(4)
    red_4(0)
    backward(3)
    for q in range(4, NZ):
        backward(q)

    grad = gacc[...].astype(BF)
    red_0(1, grad)
    for step in (red_1, red_2, red_3, red_4):
        step(1)

    for ox, oc in FAR_FIRST:
        f_copy(ox, oc).wait_send()
    for o in range(1, NX):
        px_copy(o).wait_send()
        for oy in range(1, NY):
            py_copy(o, oy).wait_send()
    for o in range(NX):
        pc_copy(o).wait_send()
    for o in range(1, NY):
        l_copy(o).wait_send()
    for t in range(NZ):
        for o in range(1, NY):
            yf_copy(t, o).wait_send()
            for u in range(2):
                yb_copy(t, o, u).wait_send()
        if 3 <= t < NZ - 1:
            zf_copy(t).wait_send()
    for way in range(2):
        zx_copy(way).wait_send()
        zy_copy(way).wait_send()
        for k in range(NZ // 2):
            for u in range(2):
                ag_copy(k, way, u).wait_send()
    for h in range(2):
        for o in range(NX):
            rc_copy(h, o).wait_send()
        for o in range(1, NX):
            rx_copy(h, o).wait_send()
        for buf, sem in ((ry, ry_s), (yg, yg_s)):
            pltpu.make_async_copy(others(buf, h), others(buf, h), sem.at[h]).wait()


def local(feats, projection, tiles, slot_owner, slot_block, source_block, counts, out_grad):
    vmem = pl.BlockSpec(memory_space=pltpu.VMEM)
    hbm = pl.BlockSpec(memory_space=pl.ANY)
    dma = pltpu.SemaphoreType.DMA
    scratch = [
        pltpu.VMEM((NF, ROWS, BLK), BF),
        pltpu.VMEM((NX, NC, BLK, 2 * HID), BF),
        pltpu.VMEM((SLOTS, KB, BLK, BLK), BF),
        pltpu.VMEM((ROWS, HID), BF),
        pltpu.VMEM((NB, BLK, HID), BF),
        pltpu.VMEM((ROWS, HID), BF),
        pltpu.VMEM((NF, BLK, ROWS), BF),
        pltpu.VMEM((SLOTS, NB * BLK, BLK), BF),
        pltpu.VMEM((CAP + 1, ND, 128), jnp.int32),
        pltpu.SMEM((CAP + 1, ND, 128), jnp.int32),
        pltpu.VMEM((ROWS, HID), F32),
        pltpu.VMEM((NY, CAP, NZ, HID), jnp.int32),
        pltpu.VMEM((NY, CAP, NZ, HID), jnp.int32),
        pltpu.VMEM((NZ, NY, CAP, BLK, HID), BF),
        pltpu.VMEM((NZ, NY, CAP, BLK, HID), BF),
        pltpu.VMEM((NZ, NB, BLK, HID), BF),
        pltpu.VMEM((NZ, NB, BLK, HID), BF),
        pltpu.VMEM((2, 2, BLK, HID), BF),
        pltpu.VMEM((2, NB, BLK, HID), BF),
        pltpu.VMEM((ROWS, HID), F32),
        pltpu.VMEM((NZ, NB, 2, HALF, HID), BF),
        pltpu.VMEM((NZ, NY, CAP, 2, HALF, HID), BF),
        pltpu.VMEM((NZ, NY, CAP, 2, HALF, HID), BF),
        pltpu.VMEM((ROWS, HID), BF),
        pltpu.VMEM((ROWS, HID), F32),
        pltpu.VMEM((2, NX, BLK, HID), F32),
        pltpu.VMEM((2, NX, BLK, HID), F32),
        pltpu.VMEM((2, NX, BLK, HID), F32),
        pltpu.VMEM((2, NX, BLK, HID), F32),
        pltpu.VMEM((2, ND, 8, 128), F32),
        pltpu.VMEM((2, ND, 8, 128), F32),
        pltpu.VMEM((2, 8, 128), F32),
        pltpu.VMEM((2, ND, 8, 128), F32),
        dma((5,)),
        dma((NF,)), dma((NF,)), dma((NX,)), dma((NX,)), dma((NX, NY)), dma((NX, NY)),
        dma((NX,)), dma((NX,)), dma((NY,)), dma((NY,)),
        dma((NZ, NY)), dma((NZ, NY)), dma((NZ,)), dma((NZ,)), dma((2,)), dma((2,)), dma((2,)), dma((2,)),
        dma((NZ, 2)), dma((NZ, 2)), dma((NZ, NY, 2)), dma((NZ, NY, 2)),
        dma((2, NX)), dma((2, NX)), dma((2, NX)), dma((2, NX)),
        dma((2,)), dma((2,)), dma((2,)), dma((2,)),
    ]
    return pl.pallas_call(
        main_kernel,
        out_shape=(
            jax.ShapeDtypeStruct((ROWS, HID), BF),
            jax.ShapeDtypeStruct((BLK, 2 * HID), F32),
        ),
        in_specs=[vmem] * 4 + [hbm] * 4,
        out_specs=[vmem] * 2,
        scratch_shapes=scratch,
        compiler_params=pltpu.CompilerParams(
            collective_id=0, has_side_effects=True, vmem_limit_bytes=60 << 20
        ),
    )(
        slot_owner.reshape(1, SLOTS),
        slot_block.reshape(1, SLOTS),
        source_block.T,
        counts.reshape(NB, BLK),
        feats.reshape(NF, ROWS, BLK),
        projection,
        tiles,
        out_grad,
    )


def solution(mesh):
    placed = (
        P("dom", "feat"),
        P("feat", None),
        P(("dom", "feat"), None, None, None),
        P(("dom", "feat"), None),
        P(("dom", "feat"), None),
        P(("dom", "feat"), None),
        P(("dom", "feat")),
        P(("dom", "feat"), None),
    )
    return jax.shard_map(
        local,
        mesh=mesh,
        in_specs=placed,
        out_specs=(P(("dom", "feat"), None), P("feat", None)),
        check_vma=False,
    )
```

```python
import jax
import jax.numpy as jnp
from jax import lax
from jax.experimental import pallas as pl
from jax.experimental.pallas import tpu as pltpu
from jax.sharding import PartitionSpec as P

MESH = pl.DeviceIdType.MESH
NY, NZ, NX, NC = 4, 8, 4, 2
NF = NX * NC
ND = NY * NZ
FAR_FIRST = ((2, 0), (2, 1), (1, 0), (3, 0), (1, 1), (3, 1), (0, 1))
NEAR_FIRST = FAR_FIRST[::-1]
PLANE = sorted(
    [(oy, oz) for oy in range(NY) for oz in range(NZ) if oy or oz],
    key=lambda o: (-min(o[0], NY - o[0]) - min(o[1], NZ - o[1]), o),
)
BLK = 128
HALF = 64
NB = 4
HID = 256
ROWS = NB * BLK
KB = 4
SLOTS = 32
CAP = 2
BF, F32 = jnp.bfloat16, jnp.float32


def main_kernel(
    owner, block, source, counts, feats, proj, tiles, out_grad,
    act_out, wg_out,
    fb, pb, tb, ogb, nb, selfb, ftb, wt, tabv, tabs, inv_deg,
    ls, lr, cs, yr, ms, zr, zx, zy, sm,
    ga, bs, br, gs, gacc,
    pw, rc, x1, rx, y1, ry, yt, yg,
    loc_sem, f_s, f_r, px_s, px_r, py_s, py_r, pc_s, pc_r, l_s, l_r,
    yf_s, yf_r, zf_s, zf_r, zx_s, zx_r, zy_s, zy_r, ag_s, ag_r, yb_s, yb_r,
    rc_s, rc_r, rx_s, rx_r, ry_s, ry_r, yg_s, yg_r,
):
    d = lax.axis_index("dom")
    f = lax.axis_index("feat")
    y, z = d // NZ, d % NZ
    x, c = f // NC, f % NC

    def to_feat(g):
        return (d, g)

    def to_yz(yy, zz):
        return (yy * NZ + zz, f)

    def remote(a, b, s, r, dev):
        return pltpu.make_async_remote_copy(
            src_ref=a, dst_ref=b, send_sem=s, recv_sem=r, device_id=dev, device_id_type=MESH
        )

    own_f = pltpu.make_async_copy(feats.at[f], fb.at[f], loc_sem.at[0])
    own_p = pltpu.make_async_copy(proj, pb.at[x, c], loc_sem.at[1])
    own_t = pltpu.make_async_copy(tiles, tb, loc_sem.at[2])
    own_g = pltpu.make_async_copy(out_grad, ogb, loc_sem.at[3])
    own_f.start()
    own_p.start()

    barrier = pltpu.get_barrier_semaphore()
    for o in range(1, NF):
        pl.semaphore_signal(barrier, inc=1, device_id=to_feat((f + o) % NF), device_id_type=MESH)
    for o in range(1, NY):
        pl.semaphore_signal(barrier, inc=1, device_id=to_yz((y + o) % NY, z), device_id_type=MESH)
    for o in (1, 2, NZ - 2, NZ - 1):
        pl.semaphore_signal(barrier, inc=1, device_id=to_yz(y, (z + o) % NZ), device_id_type=MESH)
    pl.semaphore_wait(barrier, NF + NY + 2)

    def f_copy(ox, oc):
        g = ((x + ox) % NX) * NC + (c + oc) % NC
        back = ((NX - ox) % NX) * NC + oc
        return remote(feats.at[g], fb.at[f], f_s.at[ox * NC + oc], f_r.at[back], to_feat(g))

    sibling = to_feat(x * NC + 1 - c)
    quarter = pl.ds(pl.multiple_of(y * (BLK // NY), BLK // NY), BLK // NY)

    def px_copy(o):
        return remote(
            proj.at[quarter], pb.at[x, c, quarter], px_s.at[o], px_r.at[NX - o],
            to_feat(((x + o) % NX) * NC + c),
        )

    def py_copy(o, oy):
        piece = pb.at[(x + o) % NX, c, quarter]
        return remote(
            piece, piece, py_s.at[o, oy], py_r.at[o, NY - oy], to_yz((y + oy) % NY, z)
        )

    def pc_copy(o):
        shard = pb.at[(x + o) % NX, c]
        return remote(shard if o else proj, shard, pc_s.at[o], pc_r.at[o], sibling)

    for o in (2, 1, 3):
        px_copy(o).start()
    for ox, oc in FAR_FIRST:
        f_copy(ox, oc).start()
    pc_copy(0).start()
    own_t.start()
    own_g.start()

    o_at = lax.broadcasted_iota(jnp.int32, (ND, SLOTS), 0)
    s_at = lax.broadcasted_iota(jnp.int32, (ND, SLOTS), 1)
    named = owner[...] == o_at
    before = jnp.dot(
        named.astype(BF), (o_at < s_at).astype(BF), preferred_element_type=F32
    )
    lane = lax.broadcasted_iota(jnp.int32, (ND, 128), 1)
    for i in range(CAP):
        here = named & (before == float(i))
        slot = jnp.sum(jnp.where(here, s_at.astype(F32), 0.0), axis=1, keepdims=True)
        label = jnp.sum(
            jnp.where(here, block[...].astype(F32) + 1.0, 0.0), axis=1, keepdims=True
        )
        tabv[i] = jnp.where(lane == 0, slot, 0.0).astype(jnp.int32)
        rows = jnp.broadcast_to((label - 1.0).astype(jnp.int32), (ND, HID))
        ls[:, i] = rows.reshape(NY, NZ, HID)
    picks = jnp.zeros((SLOTS, 128), F32)
    for k in range(KB):
        column = jnp.sum(
            jnp.where(o_at == s_at, source[k : k + 1, :].astype(F32), 0.0), axis=1, keepdims=True
        )
        picks = picks + jnp.where(lane == k, column, 0.0)
    tabv[CAP] = picks.astype(jnp.int32)
    table = pltpu.make_async_copy(tabv, tabs, loc_sem.at[4])
    table.start()

    def l_copy(o):
        yy = (y + o) % NY
        return remote(ls.at[yy], lr.at[NY - o], l_s.at[o], l_r.at[NY - o], to_yz(yy, z))

    for o in range(1, NY):
        l_copy(o).start()
    lr[0] = ls[y]

    for o in (1, 3, 2):
        piece = pb.at[(x + o) % NX, c, quarter]
        pltpu.make_async_copy(piece, piece, px_r.at[o]).wait()
        for oy in range(1, NY):
            py_copy(o, oy).start()

    diagonal = lax.broadcasted_iota(jnp.int32, (BLK, BLK), 0) == lax.broadcasted_iota(
        jnp.int32, (BLK, BLK), 1
    )
    for b in range(NB):
        column = jnp.sum(
            jnp.where(diagonal, counts[b : b + 1, :].astype(F32), 0.0), axis=1, keepdims=True
        )
        inv_deg[b * BLK : (b + 1) * BLK, :] = jnp.broadcast_to(1.0 / column, (BLK, HID))

    own_p.wait()
    for o in (1, 3, 2):
        for oy in range(1, NY):
            theirs = pl.ds(pl.multiple_of(((y + oy) % NY) * (BLK // NY), BLK // NY), BLK // NY)
            piece = pb.at[(x + o) % NX, c, theirs]
            pltpu.make_async_copy(piece, piece, py_r.at[o, oy]).wait()
        pc_copy(o).start()
    table.wait()

    own_f.wait()
    for o in range(NX):
        shard = pb.at[(x + o) % NX, 1 - c]
        pltpu.make_async_copy(shard, shard, pc_r.at[o]).wait()
    sm[...] = jnp.dot(fb[f], pb[x, c, :, :HID], preferred_element_type=F32)
    for ox, oc in NEAR_FIRST:
        xx, cc = (x + ox) % NX, (c + oc) % NC
        g = xx * NC + cc
        pltpu.make_async_copy(fb.at[g], fb.at[g], f_r.at[ox * NC + oc]).wait()
        sm[...] += jnp.dot(fb[g], pb[xx, cc, :, :HID], preferred_element_type=F32)
    nb[...] = sm[...].astype(BF).reshape(NB, BLK, HID)
    own_t.wait()

    def far_first(t):
        return (z + NZ // 2 + (1 - 2 * (t % 2)) * ((t + 1) // 2)) % NZ

    def near_first(q):
        return (z + NZ + (1 - 2 * (q % 2)) * ((q + 1) // 2)) % NZ

    def yf_copy(t, o):
        return remote(
            cs.at[t, o], yr.at[t, NY - o], yf_s.at[t, o], yf_r.at[t, NY - o], to_yz((y + o) % NY, z)
        )

    def slot_at(i, at):
        return jnp.clip(tabs[i, at, 0], 0, SLOTS - 1)

    def source_at(s, k):
        return jnp.clip(tabs[CAP, s, k], 0, NB - 1)

    def contribute(t, carry):
        zz = far_first(t)
        for o in range(1, NY + 1):
            r = o % NY
            yy = (y + r) % NY
            for i in range(CAP):
                s = slot_at(i, yy * NZ + zz)
                total = None
                for k in range(0, KB, 2):
                    left = jnp.concatenate([tb[s, k], tb[s, k + 1]], axis=1)
                    right = jnp.concatenate(
                        [nb[source_at(s, k)], nb[source_at(s, k + 1)]], axis=0
                    )
                    part = jnp.dot(left, right, preferred_element_type=F32)
                    total = part if total is None else total + part
                if r:
                    cs[t, r, i] = total.astype(BF)
                else:
                    yr[t, 0, i] = total.astype(BF)
            if r:
                yf_copy(t, r).start()
        return carry

    lax.fori_loop(0, NZ, contribute, 0)

    sm[...] = jnp.dot(fb[f], pb[x, c, :, HID:], preferred_element_type=F32)
    for ox, oc in NEAR_FIRST:
        xx, cc = (x + ox) % NX, (c + oc) % NC
        sm[...] += jnp.dot(fb[xx * NC + cc], pb[xx, cc, :, HID:], preferred_element_type=F32)
    selfb[...] = sm[...].astype(BF)
    for o in range(1, NY):
        pltpu.make_async_copy(lr.at[o], lr.at[o], l_r.at[o]).wait()

    def along_z(o):
        return to_yz(y, (z + o + NZ) % NZ)

    def zf_copy(t):
        return remote(ms.at[t], zr.at[t], zf_s.at[t], zf_r.at[t], along_z({3: 2, 4: -2, 5: 1, 6: -1}[t]))

    def zx_copy(way):
        half = ms.at[0, pl.ds(2 * way, 2)]
        return remote(half, zx.at[way], zx_s.at[way], zx_r.at[way], along_z((2, -2)[way]))

    def zy_copy(way):
        return remote(ms.at[1 + way], zy.at[way], zy_s.at[way], zy_r.at[way], along_z((1, -1)[way]))

    def merge(t):
        zz = far_first(t)
        for o in range(1, NY):
            pltpu.make_async_copy(yr.at[t, o], yr.at[t, o], yf_r.at[t, o]).wait()
        way = t - 3
        if way in (0, 1):
            zx_copy(way).wait_recv()
            zy_copy(way).wait_recv()

        def rows(n, inner):
            part = pl.ds(pl.multiple_of(n * 32, 32), 32)
            sums = [jnp.zeros((32, HID), F32) for b in range(NB)]
            for o in range(NY):
                for i in range(CAP):
                    row = jnp.broadcast_to(lr[o, i, pl.ds(zz, 1), :], (32, HID))
                    value = yr[t, o, i, part, :].astype(F32)
                    for b in range(NB):
                        sums[b] = sums[b] + jnp.where(row == b, value, 0.0)
            for b in range(NB):
                if way in (0, 1):
                    sums[b] = sums[b] + zy[way, b, part, :].astype(F32)
                    if b // 2 == way:
                        sums[b] = sums[b] + zx[way, b % 2, part, :].astype(F32)
                if t < NZ - 1:
                    ms[t, b, part, :] = sums[b].astype(BF)
                else:
                    sm[pl.ds(pl.multiple_of(b * BLK + n * 32, 32), 32), :] = sums[b]
            return inner

        lax.fori_loop(0, BLK // 32, rows, 0)
        if t == 0:
            zx_copy(0).start()
            zx_copy(1).start()
        elif t < 3:
            zy_copy(t - 1).start()
        elif t < NZ - 1:
            zf_copy(t).start()

        def turn(n, inner):
            s = t * (SLOTS // (NZ - 1)) + n
            parts = [tb[s, k].astype(F32) for k in range(KB)]
            for b in range(NB):
                total = jnp.zeros((BLK, BLK), F32)
                for k in range(KB):
                    total = total + jnp.where(source_at(s, k) == b, parts[k], 0.0)
                wt[s, pl.ds(b * BLK, BLK), :] = total.astype(BF).T
            return inner

        if t < NZ - 1:
            most = SLOTS // (NZ - 1)
            lax.fori_loop(0, most if t < NZ - 2 else SLOTS - t * most, turn, 0)
            for g in (t, NZ - 1) if t == NZ - 2 else (t,):
                for b in range(NB):
                    ftb[g, :, pl.ds(b * BLK, BLK)] = fb[g, pl.ds(b * BLK, BLK), :].T

    for t in range(NZ):
        merge(t)
    own_g.wait()

    for t in range(3, NZ - 1):
        pltpu.make_async_copy(zr.at[t], zr.at[t], zf_r.at[t]).wait()

        def add(b, inner):
            rows = pl.ds(pl.multiple_of(b * BLK, BLK), BLK)
            sm[rows, :] = sm[rows, :] + zr[t, b].astype(F32)
            return inner

        lax.fori_loop(0, NB, add, 0)

    def pointwise(u):
        def some(n, carry):
            b, m = n // 2, n % 2
            rows = pl.ds(pl.multiple_of(b * BLK + u * HALF + m * 32, 32), 32)
            inv = inv_deg[rows, :]
            preact = sm[rows, :] * inv + selfb[rows, :].astype(F32)
            sigma = jax.nn.sigmoid(preact)
            act_out[rows, :] = (preact * sigma).astype(BF)
            grad_pre = ogb[rows, :].astype(F32) * sigma * (1.0 + preact * (1.0 - sigma))
            gs[rows, :] = grad_pre.astype(BF)
            ga[0, b, u, pl.ds(pl.multiple_of(m * 32, 32), 32), :] = (grad_pre * inv).astype(BF)
            return carry

        lax.fori_loop(0, NB * 2, some, 0)

    up, down = to_yz(y, (z + 1) % NZ), to_yz(y, (z + NZ - 1) % NZ)

    def ag_copy(k, way, u):
        q = 2 * k - 1 + way if k else 0
        blocks = pl.ds(0, NB) if k < NZ // 2 - 1 else pl.ds(2 * way, 2)
        to = 2 * k + 1 + way if k < NZ // 2 - 1 else NZ - 1
        return remote(
            ga.at[q, blocks, u], ga.at[to, blocks, u],
            ag_s.at[2 * k + way, u], ag_r.at[2 * k + way, u], (up, down)[way],
        )

    def yb_copy(q, o, u):
        return remote(
            bs.at[q, o, :, u], br.at[q, NY - o, :, u], yb_s.at[q, o, u], yb_r.at[q, NY - o, u],
            to_yz((y + o) % NY, z),
        )

    def answer(q, u):
        zz = near_first(q)

        def rows(n, inner):
            part = pl.ds(pl.multiple_of(n * 32, 32), 32)
            blocks = [ga[q, b, u, part, :].astype(F32) for b in range(NB)]
            for o in range(NY):
                for i in range(CAP):
                    row = jnp.broadcast_to(lr[o, i, pl.ds(zz, 1), :], (32, HID))
                    value = jnp.zeros((32, HID), F32)
                    for b in range(NB):
                        value = jnp.where(row == b, blocks[b], value)
                    if o:
                        bs[q, o, i, u, part, :] = value.astype(BF)
                    else:
                        br[q, 0, i, u, part, :] = value.astype(BF)
            return inner

        lax.fori_loop(0, HALF // 32, rows, 0)
        for o in range(1, NY):
            yb_copy(q, o, u).start()

    def backward(q):
        zz = near_first(q)
        for o in range(1, NY):
            for u in range(2):
                piece = br.at[q, o, :, u]
                pltpu.make_async_copy(piece, piece, yb_r.at[q, o, u]).wait()

        def pair(r, carry):
            at = ((y + r) % NY) * NZ + zz
            left = jnp.concatenate([wt[slot_at(0, at)], wt[slot_at(1, at)]], axis=1)
            right = br[q, r].reshape(CAP * BLK, HID)
            gacc[...] += jnp.dot(left, right, preferred_element_type=F32)
            return carry

        lax.fori_loop(0, NY, pair, 0)

    def rc_copy(h, o):
        xx = (x + o) % NX
        return remote(pw.at[h, xx], rc.at[h, xx], rc_s.at[h, o], rc_r.at[h, o], sibling)

    def rx_copy(h, o):
        xx = (x + o) % NX
        return remote(
            x1.at[h, xx], rx.at[h, NX - o], rx_s.at[h, o], rx_r.at[h, NX - o], to_feat(xx * NC + c)
        )

    def plane_copies(a, b, s, r, h, per_device):
        for oy, oz in PLANE:
            e = ((y + oy) % NY) * NZ + (z + oz) % NZ
            back = ((NY - oy) % NY) * NZ + (NZ - oz) % NZ
            part = a.at[h, e] if per_device else a.at[h]
            remote(part, b.at[h, back], s.at[h], r.at[h], (e, f)).start()

    def red_0(h, grad):
        for o in (2, 1, 3, 0):
            xx = (x + o) % NX
            pw[h, xx] = jnp.dot(ftb[xx * NC + 1 - c], grad, preferred_element_type=F32)
            rc_copy(h, o).start()
        for o in (2, 1, 3, 0):
            xx = (x + o) % NX
            x1[h, xx] = jnp.dot(ftb[xx * NC + c], grad, preferred_element_type=F32)

    def red_1(h):
        for o in (2, 1, 3, 0):
            xx = (x + o) % NX
            rc_copy(h, o).wait_recv()
            x1[h, xx] = x1[h, xx] + rc[h, xx]
            if o:
                rx_copy(h, o).start()

    def red_2(h):
        total = x1[h, x]
        for o in (1, 3, 2):
            pltpu.make_async_copy(rx.at[h, o], rx.at[h, o], rx_r.at[h, o]).wait()
            total = total + rx[h, o]
        for n in range(ND):
            r, q = n // 2, n % 2
            y1[h, n] = total[r * 8 : r * 8 + 8, q * 128 : q * 128 + 128]

    def red_3(h):
        plane_copies(y1, ry, ry_s, ry_r, h, True)

    def others(buf, h):
        return buf.at[h, pl.ds(1, ND - 1)]

    def red_4(h):
        total = y1[h, d]
        pltpu.make_async_copy(others(ry, h), others(ry, h), ry_r.at[h]).wait()
        for o in range(1, ND):
            total = total + ry[h, o]
        yt[h] = total
        yg[h, 0] = total
        plane_copies(yt, yg, yg_s, yg_r, h, False)

    def red_5(h):
        pltpu.make_async_copy(others(yg, h), others(yg, h), yg_r.at[h]).wait()
        for n in range(ND):
            r, q = n // 2, n % 2
            back = ((n // NZ - y + NY) % NY) * NZ + (n % NZ - z + NZ) % NZ
            wg_out[pl.ds(r * 8, 8), pl.ds(HID * (1 - h) + q * 128, 128)] = yg[h, back]

    gacc[...] = jnp.zeros_like(gacc)
    for u in range(2):
        pointwise(u)
        for way in range(2):
            ag_copy(0, way, u).start()
        answer(0, u)

    def pass_on(k):
        for u in range(2):
            for way in range(2):
                ag_copy(k - 1, way, u).wait_recv()
                if k < NZ // 2:
                    ag_copy(k, way, u).start()
            if k < NZ // 2:
                answer(2 * k - 1, u)
                answer(2 * k, u)
            else:
                answer(NZ - 1, u)

    red_0(0, gs[...])
    pass_on(1)
    red_1(0)
    backward(0)
    pass_on(2)
    red_2(0)
    backward(1)
    pass_on(3)
    backward(2)
    pass_on(4)
    backward(3)
    for q in range(4, NZ):
        backward(q)

    grad = gacc[...].astype(BF)
    red_0(1, grad)
    red_1(1)
    red_3(0)
    red_2(1)
    red_3(1)
    red_4(0)
    red_4(1)
    red_5(0)
    red_5(1)

    for ox, oc in FAR_FIRST:
        f_copy(ox, oc).wait_send()
    for o in range(1, NX):
        px_copy(o).wait_send()
        for oy in range(1, NY):
            py_copy(o, oy).wait_send()
    for o in range(NX):
        pc_copy(o).wait_send()
    for o in range(1, NY):
        l_copy(o).wait_send()
    for t in range(NZ):
        for o in range(1, NY):
            yf_copy(t, o).wait_send()
            for u in range(2):
                yb_copy(t, o, u).wait_send()
        if 3 <= t < NZ - 1:
            zf_copy(t).wait_send()
    for way in range(2):
        zx_copy(way).wait_send()
        zy_copy(way).wait_send()
        for k in range(NZ // 2):
            for u in range(2):
                ag_copy(k, way, u).wait_send()
    for h in range(2):
        for o in range(NX):
            rc_copy(h, o).wait_send()
        for o in range(1, NX):
            rx_copy(h, o).wait_send()
        for buf, sem in ((ry, ry_s), (yg, yg_s)):
            pltpu.make_async_copy(others(buf, h), others(buf, h), sem.at[h]).wait()


def local(feats, projection, tiles, slot_owner, slot_block, source_block, counts, out_grad):
    vmem = pl.BlockSpec(memory_space=pltpu.VMEM)
    hbm = pl.BlockSpec(memory_space=pl.ANY)
    dma = pltpu.SemaphoreType.DMA
    scratch = [
        pltpu.VMEM((NF, ROWS, BLK), BF),
        pltpu.VMEM((NX, NC, BLK, 2 * HID), BF),
        pltpu.VMEM((SLOTS, KB, BLK, BLK), BF),
        pltpu.VMEM((ROWS, HID), BF),
        pltpu.VMEM((NB, BLK, HID), BF),
        pltpu.VMEM((ROWS, HID), BF),
        pltpu.VMEM((NF, BLK, ROWS), BF),
        pltpu.VMEM((SLOTS, NB * BLK, BLK), BF),
        pltpu.VMEM((CAP + 1, ND, 128), jnp.int32),
        pltpu.SMEM((CAP + 1, ND, 128), jnp.int32),
        pltpu.VMEM((ROWS, HID), F32),
        pltpu.VMEM((NY, CAP, NZ, HID), jnp.int32),
        pltpu.VMEM((NY, CAP, NZ, HID), jnp.int32),
        pltpu.VMEM((NZ, NY, CAP, BLK, HID), BF),
        pltpu.VMEM((NZ, NY, CAP, BLK, HID), BF),
        pltpu.VMEM((NZ, NB, BLK, HID), BF),
        pltpu.VMEM((NZ, NB, BLK, HID), BF),
        pltpu.VMEM((2, 2, BLK, HID), BF),
        pltpu.VMEM((2, NB, BLK, HID), BF),
        pltpu.VMEM((ROWS, HID), F32),
        pltpu.VMEM((NZ, NB, 2, HALF, HID), BF),
        pltpu.VMEM((NZ, NY, CAP, 2, HALF, HID), BF),
        pltpu.VMEM((NZ, NY, CAP, 2, HALF, HID), BF),
        pltpu.VMEM((ROWS, HID), BF),
        pltpu.VMEM((ROWS, HID), F32),
        pltpu.VMEM((2, NX, BLK, HID), F32),
        pltpu.VMEM((2, NX, BLK, HID), F32),
        pltpu.VMEM((2, NX, BLK, HID), F32),
        pltpu.VMEM((2, NX, BLK, HID), F32),
        pltpu.VMEM((2, ND, 8, 128), F32),
        pltpu.VMEM((2, ND, 8, 128), F32),
        pltpu.VMEM((2, 8, 128), F32),
        pltpu.VMEM((2, ND, 8, 128), F32),
        dma((5,)),
        dma((NF,)), dma((NF,)), dma((NX,)), dma((NX,)), dma((NX, NY)), dma((NX, NY)),
        dma((NX,)), dma((NX,)), dma((NY,)), dma((NY,)),
        dma((NZ, NY)), dma((NZ, NY)), dma((NZ,)), dma((NZ,)), dma((2,)), dma((2,)), dma((2,)), dma((2,)),
        dma((NZ, 2)), dma((NZ, 2)), dma((NZ, NY, 2)), dma((NZ, NY, 2)),
        dma((2, NX)), dma((2, NX)), dma((2, NX)), dma((2, NX)),
        dma((2,)), dma((2,)), dma((2,)), dma((2,)),
    ]
    return pl.pallas_call(
        main_kernel,
        out_shape=(
            jax.ShapeDtypeStruct((ROWS, HID), BF),
            jax.ShapeDtypeStruct((BLK, 2 * HID), F32),
        ),
        in_specs=[vmem] * 4 + [hbm] * 4,
        out_specs=[vmem] * 2,
        scratch_shapes=scratch,
        compiler_params=pltpu.CompilerParams(
            collective_id=0, has_side_effects=True, vmem_limit_bytes=60 << 20
        ),
    )(
        slot_owner.reshape(1, SLOTS),
        slot_block.reshape(1, SLOTS),
        source_block.T,
        counts.reshape(NB, BLK),
        feats.reshape(NF, ROWS, BLK),
        projection,
        tiles,
        out_grad,
    )


def solution(mesh):
    placed = (
        P("dom", "feat"),
        P("feat", None),
        P(("dom", "feat"), None, None, None),
        P(("dom", "feat"), None),
        P(("dom", "feat"), None),
        P(("dom", "feat"), None),
        P(("dom", "feat")),
        P(("dom", "feat"), None),
    )
    return jax.shard_map(
        local,
        mesh=mesh,
        in_specs=placed,
        out_specs=(P(("dom", "feat"), None), P("feat", None)),
        check_vma=False,
    )
```

```python
import jax
import jax.numpy as jnp
from jax import lax
from jax.experimental import pallas as pl
from jax.experimental.pallas import tpu as pltpu
from jax.sharding import PartitionSpec as P

MESH = pl.DeviceIdType.MESH
NY, NZ, NX, NC = 4, 8, 4, 2
NF = NX * NC
ND = NY * NZ
FAR_FIRST = ((2, 0), (2, 1), (1, 0), (3, 0), (1, 1), (3, 1), (0, 1))
ARRIVAL = ((0, 1), (1, 0), (3, 0), (1, 1), (3, 1), (2, 0), (2, 1))
PLANE = sorted(
    [(oy, oz) for oy in range(NY) for oz in range(NZ) if oy or oz],
    key=lambda o: (-min(o[0], NY - o[0]) - min(o[1], NZ - o[1]), o),
)
BLK = 128
HALF = 64
NB = 4
HID = 256
ROWS = NB * BLK
KB = 4
SLOTS = 32
CAP = 2
BF, F32 = jnp.bfloat16, jnp.float32


def main_kernel(
    owner, block, source, counts, feats, proj, tiles, out_grad,
    act_out, wg_out,
    fb, pb, tb, ogb, nb, selfb, ftb, wt, tabv, tabs, inv_deg,
    ls, lr, cs, yr, ms, zr, zx, zy, sm,
    ga, bs, br, gs, gacc,
    pw, rc, x1, rx, xs, y1, ry, yt, yg,
    loc_sem, f_s, f_r, px_s, px_r, py_s, py_r, pc_s, pc_r, l_s, l_r,
    yf_s, yf_r, zf_s, zf_r, zx_s, zx_r, zy_s, zy_r, ag_s, ag_r, yb_s, yb_r,
    rc_s, rc_r, rx_s, rx_r, ry_s, ry_r, yg_s, yg_r,
):
    d = lax.axis_index("dom")
    f = lax.axis_index("feat")
    y, z = d // NZ, d % NZ
    x, c = f // NC, f % NC

    def to_feat(g):
        return (d, g)

    def to_yz(yy, zz):
        return (yy * NZ + zz, f)

    def remote(a, b, s, r, dev):
        return pltpu.make_async_remote_copy(
            src_ref=a, dst_ref=b, send_sem=s, recv_sem=r, device_id=dev, device_id_type=MESH
        )

    own_f = pltpu.make_async_copy(feats.at[f], fb.at[f], loc_sem.at[0])
    own_p = pltpu.make_async_copy(proj, pb.at[x, c], loc_sem.at[1])
    own_t = pltpu.make_async_copy(tiles, tb, loc_sem.at[2])
    own_g = pltpu.make_async_copy(out_grad, ogb, loc_sem.at[3])
    own_f.start()
    own_p.start()

    barrier = pltpu.get_barrier_semaphore()
    for o in range(1, NF):
        pl.semaphore_signal(barrier, inc=1, device_id=to_feat((f + o) % NF), device_id_type=MESH)
    for o in range(1, NY):
        pl.semaphore_signal(barrier, inc=1, device_id=to_yz((y + o) % NY, z), device_id_type=MESH)
    for o in (1, 2, NZ - 2, NZ - 1):
        pl.semaphore_signal(barrier, inc=1, device_id=to_yz(y, (z + o) % NZ), device_id_type=MESH)
    pl.semaphore_wait(barrier, NF + NY + 2)

    def f_copy(ox, oc):
        g = ((x + ox) % NX) * NC + (c + oc) % NC
        back = ((NX - ox) % NX) * NC + oc
        return remote(feats.at[g], fb.at[f], f_s.at[ox * NC + oc], f_r.at[back], to_feat(g))

    sibling = to_feat(x * NC + 1 - c)
    quarter = pl.ds(pl.multiple_of(y * (BLK // NY), BLK // NY), BLK // NY)

    def px_copy(o):
        return remote(
            proj.at[quarter], pb.at[x, c, quarter], px_s.at[o], px_r.at[NX - o],
            to_feat(((x + o) % NX) * NC + c),
        )

    def py_copy(o, oy):
        piece = pb.at[(x + o) % NX, c, quarter]
        return remote(
            piece, piece, py_s.at[o, oy], py_r.at[o, NY - oy], to_yz((y + oy) % NY, z)
        )

    def pc_copy(o):
        shard = pb.at[(x + o) % NX, c]
        return remote(shard if o else proj, shard, pc_s.at[o], pc_r.at[o], sibling)

    for o in (2, 1, 3):
        px_copy(o).start()
    for ox, oc in FAR_FIRST:
        f_copy(ox, oc).start()
    pc_copy(0).start()
    own_t.start()
    own_g.start()

    o_at = lax.broadcasted_iota(jnp.int32, (ND, SLOTS), 0)
    s_at = lax.broadcasted_iota(jnp.int32, (ND, SLOTS), 1)
    named = owner[...] == o_at
    before = jnp.dot(
        named.astype(BF), (o_at < s_at).astype(BF), preferred_element_type=F32
    )
    lane = lax.broadcasted_iota(jnp.int32, (ND, 128), 1)
    for i in range(CAP):
        here = named & (before == float(i))
        slot = jnp.sum(jnp.where(here, s_at.astype(F32), 0.0), axis=1, keepdims=True)
        label = jnp.sum(
            jnp.where(here, block[...].astype(F32) + 1.0, 0.0), axis=1, keepdims=True
        )
        tabv[i] = jnp.where(lane == 0, slot, 0.0).astype(jnp.int32)
        rows = jnp.broadcast_to((label - 1.0).astype(jnp.int32), (ND, HID))
        ls[:, i] = rows.reshape(NY, NZ, HID)
    picks = jnp.zeros((SLOTS, 128), F32)
    for k in range(KB):
        column = jnp.sum(
            jnp.where(o_at == s_at, source[k : k + 1, :].astype(F32), 0.0), axis=1, keepdims=True
        )
        picks = picks + jnp.where(lane == k, column, 0.0)
    tabv[CAP] = picks.astype(jnp.int32)
    table = pltpu.make_async_copy(tabv, tabs, loc_sem.at[4])
    table.start()

    def l_copy(o):
        yy = (y + o) % NY
        return remote(ls.at[yy], lr.at[NY - o], l_s.at[o], l_r.at[NY - o], to_yz(yy, z))

    for o in range(1, NY):
        l_copy(o).start()
    lr[0] = ls[y]

    for o in (1, 3, 2):
        piece = pb.at[(x + o) % NX, c, quarter]
        pltpu.make_async_copy(piece, piece, px_r.at[o]).wait()
        for oy in range(1, NY):
            py_copy(o, oy).start()

    diagonal = lax.broadcasted_iota(jnp.int32, (BLK, BLK), 0) == lax.broadcasted_iota(
        jnp.int32, (BLK, BLK), 1
    )
    for b in range(NB):
        column = jnp.sum(
            jnp.where(diagonal, counts[b : b + 1, :].astype(F32), 0.0), axis=1, keepdims=True
        )
        inv_deg[b * BLK : (b + 1) * BLK, :] = jnp.broadcast_to(1.0 / column, (BLK, HID))

    own_p.wait()
    for o in (1, 3, 2):
        for oy in range(1, NY):
            theirs = pl.ds(pl.multiple_of(((y + oy) % NY) * (BLK // NY), BLK // NY), BLK // NY)
            piece = pb.at[(x + o) % NX, c, theirs]
            pltpu.make_async_copy(piece, piece, py_r.at[o, oy]).wait()
        pc_copy(o).start()
    table.wait()

    own_f.wait()
    sm[...] = jnp.dot(fb[f], pb[x, c, :, :HID], preferred_element_type=F32)
    for ox, oc in ARRIVAL:
        xx, cc = (x + ox) % NX, (c + oc) % NC
        g = xx * NC + cc
        if oc:
            shard = pb.at[xx, cc]
            pltpu.make_async_copy(shard, shard, pc_r.at[ox]).wait()
        pltpu.make_async_copy(fb.at[g], fb.at[g], f_r.at[ox * NC + oc]).wait()
        sm[...] += jnp.dot(fb[g], pb[xx, cc, :, :HID], preferred_element_type=F32)
    nb[...] = sm[...].astype(BF).reshape(NB, BLK, HID)
    own_t.wait()

    def far_first(t):
        return (z + NZ // 2 + (1 - 2 * (t % 2)) * ((t + 1) // 2)) % NZ

    def near_first(q):
        return (z + NZ + (1 - 2 * (q % 2)) * ((q + 1) // 2)) % NZ

    def yf_copy(t, o):
        return remote(
            cs.at[t, o], yr.at[t, NY - o], yf_s.at[t, o], yf_r.at[t, NY - o], to_yz((y + o) % NY, z)
        )

    def slot_at(i, at):
        return jnp.clip(tabs[i, at, 0], 0, SLOTS - 1)

    def source_at(s, k):
        return jnp.clip(tabs[CAP, s, k], 0, NB - 1)

    def contribute(t, carry):
        zz = far_first(t)
        for o in range(1, NY + 1):
            r = o % NY
            yy = (y + r) % NY
            for i in range(CAP):
                s = slot_at(i, yy * NZ + zz)
                total = None
                for k in range(0, KB, 2):
                    left = jnp.concatenate([tb[s, k], tb[s, k + 1]], axis=1)
                    right = jnp.concatenate(
                        [nb[source_at(s, k)], nb[source_at(s, k + 1)]], axis=0
                    )
                    part = jnp.dot(left, right, preferred_element_type=F32)
                    total = part if total is None else total + part
                if r:
                    cs[t, r, i] = total.astype(BF)
                else:
                    yr[t, 0, i] = total.astype(BF)
            if r:
                yf_copy(t, r).start()
        return carry

    lax.fori_loop(0, NZ, contribute, 0)

    sm[...] = jnp.dot(fb[f], pb[x, c, :, HID:], preferred_element_type=F32)
    for ox, oc in ARRIVAL:
        xx, cc = (x + ox) % NX, (c + oc) % NC
        sm[...] += jnp.dot(fb[xx * NC + cc], pb[xx, cc, :, HID:], preferred_element_type=F32)
    selfb[...] = sm[...].astype(BF)
    for o in range(1, NY):
        pltpu.make_async_copy(lr.at[o], lr.at[o], l_r.at[o]).wait()

    def along_z(o):
        return to_yz(y, (z + o + NZ) % NZ)

    def zf_copy(t):
        return remote(ms.at[t], zr.at[t], zf_s.at[t], zf_r.at[t], along_z({3: 2, 4: -2, 5: 1, 6: -1}[t]))

    def zx_copy(way):
        half = ms.at[0, pl.ds(2 * way, 2)]
        return remote(half, zx.at[way], zx_s.at[way], zx_r.at[way], along_z((2, -2)[way]))

    def zy_copy(way):
        return remote(ms.at[1 + way], zy.at[way], zy_s.at[way], zy_r.at[way], along_z((1, -1)[way]))

    def merge(t):
        zz = far_first(t)
        for o in range(1, NY):
            pltpu.make_async_copy(yr.at[t, o], yr.at[t, o], yf_r.at[t, o]).wait()
        way = t - 3
        if way in (0, 1):
            zx_copy(way).wait_recv()
            zy_copy(way).wait_recv()

        def rows(n, inner):
            part = pl.ds(pl.multiple_of(n * 32, 32), 32)
            sums = [jnp.zeros((32, HID), F32) for b in range(NB)]
            for o in range(NY):
                for i in range(CAP):
                    row = jnp.broadcast_to(lr[o, i, pl.ds(zz, 1), :], (32, HID))
                    value = yr[t, o, i, part, :].astype(F32)
                    for b in range(NB):
                        sums[b] = sums[b] + jnp.where(row == b, value, 0.0)
            for b in range(NB):
                if way in (0, 1):
                    sums[b] = sums[b] + zy[way, b, part, :].astype(F32)
                    if b // 2 == way:
                        sums[b] = sums[b] + zx[way, b % 2, part, :].astype(F32)
                if t < NZ - 1:
                    ms[t, b, part, :] = sums[b].astype(BF)
                else:
                    sm[pl.ds(pl.multiple_of(b * BLK + n * 32, 32), 32), :] = sums[b]
            return inner

        lax.fori_loop(0, BLK // 32, rows, 0)
        if t == 0:
            zx_copy(0).start()
            zx_copy(1).start()
        elif t < 3:
            zy_copy(t - 1).start()
        elif t < NZ - 1:
            zf_copy(t).start()

        def turn(n, inner):
            s = t * (SLOTS // (NZ - 1)) + n
            parts = [tb[s, k].astype(F32) for k in range(KB)]
            for b in range(NB):
                total = jnp.zeros((BLK, BLK), F32)
                for k in range(KB):
                    total = total + jnp.where(source_at(s, k) == b, parts[k], 0.0)
                wt[s, pl.ds(b * BLK, BLK), :] = total.astype(BF).T
            return inner

        if t < NZ - 1:
            most = SLOTS // (NZ - 1)
            lax.fori_loop(0, most if t < NZ - 2 else SLOTS - t * most, turn, 0)
            for g in (t, NZ - 1) if t == NZ - 2 else (t,):
                for b in range(NB):
                    ftb[g % NC, g // NC, :, pl.ds(b * BLK, BLK)] = fb[g, pl.ds(b * BLK, BLK), :].T

    for t in range(NZ):
        merge(t)
    own_g.wait()

    for t in range(3, NZ - 1):
        pltpu.make_async_copy(zr.at[t], zr.at[t], zf_r.at[t]).wait()

        def add(b, inner):
            rows = pl.ds(pl.multiple_of(b * BLK, BLK), BLK)
            sm[rows, :] = sm[rows, :] + zr[t, b].astype(F32)
            return inner

        lax.fori_loop(0, NB, add, 0)

    def pointwise(u):
        def some(n, carry):
            b, m = n // 2, n % 2
            rows = pl.ds(pl.multiple_of(b * BLK + u * HALF + m * 32, 32), 32)
            inv = inv_deg[rows, :]
            preact = sm[rows, :] * inv + selfb[rows, :].astype(F32)
            sigma = jax.nn.sigmoid(preact)
            act_out[rows, :] = (preact * sigma).astype(BF)
            grad_pre = ogb[rows, :].astype(F32) * sigma * (1.0 + preact * (1.0 - sigma))
            gs[rows, :] = grad_pre.astype(BF)
            ga[0, b, u, pl.ds(pl.multiple_of(m * 32, 32), 32), :] = (grad_pre * inv).astype(BF)
            return carry

        lax.fori_loop(0, NB * 2, some, 0)

    up, down = to_yz(y, (z + 1) % NZ), to_yz(y, (z + NZ - 1) % NZ)

    def ag_copy(k, way, u):
        q = 2 * k - 1 + way if k else 0
        blocks = pl.ds(0, NB) if k < NZ // 2 - 1 else pl.ds(2 * way, 2)
        to = 2 * k + 1 + way if k < NZ // 2 - 1 else NZ - 1
        return remote(
            ga.at[q, blocks, u], ga.at[to, blocks, u],
            ag_s.at[2 * k + way, u], ag_r.at[2 * k + way, u], (up, down)[way],
        )

    def yb_copy(q, o, u):
        return remote(
            bs.at[q, o, :, u], br.at[q, NY - o, :, u], yb_s.at[q, o, u], yb_r.at[q, NY - o, u],
            to_yz((y + o) % NY, z),
        )

    def answer(q, u):
        zz = near_first(q)

        def rows(n, inner):
            part = pl.ds(pl.multiple_of(n * 32, 32), 32)
            blocks = [ga[q, b, u, part, :].astype(F32) for b in range(NB)]
            for o in range(NY):
                for i in range(CAP):
                    row = jnp.broadcast_to(lr[o, i, pl.ds(zz, 1), :], (32, HID))
                    value = jnp.zeros((32, HID), F32)
                    for b in range(NB):
                        value = jnp.where(row == b, blocks[b], value)
                    if o:
                        bs[q, o, i, u, part, :] = value.astype(BF)
                    else:
                        br[q, 0, i, u, part, :] = value.astype(BF)
            return inner

        lax.fori_loop(0, HALF // 32, rows, 0)
        for o in range(1, NY):
            yb_copy(q, o, u).start()

    def backward(q):
        zz = near_first(q)
        for o in range(1, NY):
            for u in range(2):
                piece = br.at[q, o, :, u]
                pltpu.make_async_copy(piece, piece, yb_r.at[q, o, u]).wait()

        def pair(r, carry):
            at = ((y + r) % NY) * NZ + zz
            left = jnp.concatenate([wt[slot_at(0, at)], wt[slot_at(1, at)]], axis=1)
            right = br[q, r].reshape(CAP * BLK, HID)
            gacc[...] += jnp.dot(left, right, preferred_element_type=F32)
            return carry

        lax.fori_loop(0, NY, pair, 0)

    def rc_copy(h, o):
        xx = (x + o) % NX
        return remote(pw.at[h, xx], rc.at[h, xx], rc_s.at[h, o], rc_r.at[h, o], sibling)

    def rx_copy(h, o):
        xx = (x + o) % NX
        return remote(
            xs.at[h, xx], rx.at[h, NX - o], rx_s.at[h, o], rx_r.at[h, NX - o], to_feat(xx * NC + c)
        )

    def plane_copies(a, b, s, r, h, per_device):
        for oy, oz in PLANE:
            e = ((y + oy) % NY) * NZ + (z + oz) % NZ
            back = ((NY - oy) % NY) * NZ + (NZ - oz) % NZ
            part = a.at[h, e] if per_device else a.at[h]
            remote(part, b.at[h, back], s.at[h], r.at[h], (e, f)).start()

    def red_0(h, grad):
        def term(parity):
            left = ftb[parity].reshape(NX * BLK, ROWS)
            return jnp.dot(left, grad, preferred_element_type=F32).reshape(NX, BLK, HID)

        pw[h] = term(1 - c)
        for o in (2, 1, 3, 0):
            rc_copy(h, o).start()
        x1[h] = term(c)

    def red_1(h):
        for o in (2, 1, 3, 0):
            xx = (x + o) % NX
            rc_copy(h, o).wait_recv()
            x1[h, xx] = x1[h, xx] + rc[h, xx]
            if o:
                xs[h, xx] = x1[h, xx].astype(BF)
                rx_copy(h, o).start()

    def red_2(h):
        total = x1[h, x]
        for o in (1, 3, 2):
            pltpu.make_async_copy(rx.at[h, o], rx.at[h, o], rx_r.at[h, o]).wait()
            total = total + rx[h, o].astype(F32)
        for n in range(ND):
            r, q = n // 2, n % 2
            y1[h, n] = total[r * 8 : r * 8 + 8, q * 128 : q * 128 + 128]

    def red_3(h):
        plane_copies(y1, ry, ry_s, ry_r, h, True)

    def others(buf, h):
        return buf.at[h, pl.ds(1, ND - 1)]

    def red_4(h):
        total = y1[h, d]
        pltpu.make_async_copy(others(ry, h), others(ry, h), ry_r.at[h]).wait()
        for o in range(1, ND):
            total = total + ry[h, o]
        yt[h] = total
        yg[h, 0] = total
        plane_copies(yt, yg, yg_s, yg_r, h, False)

    def red_5(h):
        pltpu.make_async_copy(others(yg, h), others(yg, h), yg_r.at[h]).wait()
        for n in range(ND):
            r, q = n // 2, n % 2
            back = ((n // NZ - y + NY) % NY) * NZ + (n % NZ - z + NZ) % NZ
            wg_out[pl.ds(r * 8, 8), pl.ds(HID * (1 - h) + q * 128, 128)] = yg[h, back]

    gacc[...] = jnp.zeros_like(gacc)
    for u in range(2):
        pointwise(u)
        for way in range(2):
            ag_copy(0, way, u).start()
        answer(0, u)

    def pass_on(k):
        for u in range(2):
            for way in range(2):
                ag_copy(k - 1, way, u).wait_recv()
                if k < NZ // 2:
                    ag_copy(k, way, u).start()
            if k < NZ // 2:
                answer(2 * k - 1, u)
                answer(2 * k, u)
            else:
                answer(NZ - 1, u)

    red_0(0, gs[...])
    pass_on(1)
    red_1(0)
    backward(0)
    pass_on(2)
    red_2(0)
    backward(1)
    pass_on(3)
    backward(2)
    pass_on(4)
    backward(3)
    for q in range(4, NZ):
        backward(q)

    grad = gacc[...].astype(BF)
    red_0(1, grad)
    red_1(1)
    red_3(0)
    red_2(1)
    red_3(1)
    red_4(0)
    red_4(1)
    red_5(0)
    red_5(1)

    for ox, oc in FAR_FIRST:
        f_copy(ox, oc).wait_send()
    for o in range(1, NX):
        px_copy(o).wait_send()
        for oy in range(1, NY):
            py_copy(o, oy).wait_send()
    for o in range(NX):
        pc_copy(o).wait_send()
    for o in range(1, NY):
        l_copy(o).wait_send()
    for t in range(NZ):
        for o in range(1, NY):
            yf_copy(t, o).wait_send()
            for u in range(2):
                yb_copy(t, o, u).wait_send()
        if 3 <= t < NZ - 1:
            zf_copy(t).wait_send()
    for way in range(2):
        zx_copy(way).wait_send()
        zy_copy(way).wait_send()
        for k in range(NZ // 2):
            for u in range(2):
                ag_copy(k, way, u).wait_send()
    for h in range(2):
        for o in range(NX):
            rc_copy(h, o).wait_send()
        for o in range(1, NX):
            rx_copy(h, o).wait_send()
        for buf, sem in ((ry, ry_s), (yg, yg_s)):
            pltpu.make_async_copy(others(buf, h), others(buf, h), sem.at[h]).wait()


def local(feats, projection, tiles, slot_owner, slot_block, source_block, counts, out_grad):
    vmem = pl.BlockSpec(memory_space=pltpu.VMEM)
    hbm = pl.BlockSpec(memory_space=pl.ANY)
    dma = pltpu.SemaphoreType.DMA
    scratch = [
        pltpu.VMEM((NF, ROWS, BLK), BF),
        pltpu.VMEM((NX, NC, BLK, 2 * HID), BF),
        pltpu.VMEM((SLOTS, KB, BLK, BLK), BF),
        pltpu.VMEM((ROWS, HID), BF),
        pltpu.VMEM((NB, BLK, HID), BF),
        pltpu.VMEM((ROWS, HID), BF),
        pltpu.VMEM((NC, NX, BLK, ROWS), BF),
        pltpu.VMEM((SLOTS, NB * BLK, BLK), BF),
        pltpu.VMEM((CAP + 1, ND, 128), jnp.int32),
        pltpu.SMEM((CAP + 1, ND, 128), jnp.int32),
        pltpu.VMEM((ROWS, HID), F32),
        pltpu.VMEM((NY, CAP, NZ, HID), jnp.int32),
        pltpu.VMEM((NY, CAP, NZ, HID), jnp.int32),
        pltpu.VMEM((NZ, NY, CAP, BLK, HID), BF),
        pltpu.VMEM((NZ, NY, CAP, BLK, HID), BF),
        pltpu.VMEM((NZ, NB, BLK, HID), BF),
        pltpu.VMEM((NZ, NB, BLK, HID), BF),
        pltpu.VMEM((2, 2, BLK, HID), BF),
        pltpu.VMEM((2, NB, BLK, HID), BF),
        pltpu.VMEM((ROWS, HID), F32),
        pltpu.VMEM((NZ, NB, 2, HALF, HID), BF),
        pltpu.VMEM((NZ, NY, CAP, 2, HALF, HID), BF),
        pltpu.VMEM((NZ, NY, CAP, 2, HALF, HID), BF),
        pltpu.VMEM((ROWS, HID), BF),
        pltpu.VMEM((ROWS, HID), F32),
        pltpu.VMEM((2, NX, BLK, HID), F32),
        pltpu.VMEM((2, NX, BLK, HID), F32),
        pltpu.VMEM((2, NX, BLK, HID), F32),
        pltpu.VMEM((2, NX, BLK, HID), BF),
        pltpu.VMEM((2, NX, BLK, HID), BF),
        pltpu.VMEM((2, ND, 8, 128), F32),
        pltpu.VMEM((2, ND, 8, 128), F32),
        pltpu.VMEM((2, 8, 128), F32),
        pltpu.VMEM((2, ND, 8, 128), F32),
        dma((5,)),
        dma((NF,)), dma((NF,)), dma((NX,)), dma((NX,)), dma((NX, NY)), dma((NX, NY)),
        dma((NX,)), dma((NX,)), dma((NY,)), dma((NY,)),
        dma((NZ, NY)), dma((NZ, NY)), dma((NZ,)), dma((NZ,)), dma((2,)), dma((2,)), dma((2,)), dma((2,)),
        dma((NZ, 2)), dma((NZ, 2)), dma((NZ, NY, 2)), dma((NZ, NY, 2)),
        dma((2, NX)), dma((2, NX)), dma((2, NX)), dma((2, NX)),
        dma((2,)), dma((2,)), dma((2,)), dma((2,)),
    ]
    return pl.pallas_call(
        main_kernel,
        out_shape=(
            jax.ShapeDtypeStruct((ROWS, HID), BF),
            jax.ShapeDtypeStruct((BLK, 2 * HID), F32),
        ),
        in_specs=[vmem] * 4 + [hbm] * 4,
        out_specs=[vmem] * 2,
        scratch_shapes=scratch,
        compiler_params=pltpu.CompilerParams(
            collective_id=0, has_side_effects=True, vmem_limit_bytes=60 << 20
        ),
    )(
        slot_owner.reshape(1, SLOTS),
        slot_block.reshape(1, SLOTS),
        source_block.T,
        counts.reshape(NB, BLK),
        feats.reshape(NF, ROWS, BLK),
        projection,
        tiles,
        out_grad,
    )


def solution(mesh):
    placed = (
        P("dom", "feat"),
        P("feat", None),
        P(("dom", "feat"), None, None, None),
        P(("dom", "feat"), None),
        P(("dom", "feat"), None),
        P(("dom", "feat"), None),
        P(("dom", "feat")),
        P(("dom", "feat"), None),
    )
    return jax.shard_map(
        local,
        mesh=mesh,
        in_specs=placed,
        out_specs=(P(("dom", "feat"), None), P("feat", None)),
        check_vma=False,
    )
```

```python
import jax
import jax.numpy as jnp
from jax import lax
from jax.experimental import pallas as pl
from jax.experimental.pallas import tpu as pltpu
from jax.sharding import PartitionSpec as P

MESH = pl.DeviceIdType.MESH
NY, NZ, NX, NC = 4, 8, 4, 2
NF = NX * NC
ND = NY * NZ
FAR_FIRST = ((2, 0), (2, 1), (1, 0), (3, 0), (1, 1), (3, 1), (0, 1))
ARRIVAL = ((0, 1), (1, 0), (3, 0), (1, 1), (3, 1), (2, 0), (2, 1))
PLANE = sorted(
    [(oy, oz) for oy in range(NY) for oz in range(NZ) if oy or oz],
    key=lambda o: (-min(o[0], NY - o[0]) - min(o[1], NZ - o[1]), o),
)
BLK = 128
HALF = 64
NB = 4
HID = 256
ROWS = NB * BLK
KB = 4
SLOTS = 32
CAP = 2
BF, F32 = jnp.bfloat16, jnp.float32


def main_kernel(
    owner, block, source, counts, feats, proj, tiles, out_grad,
    act_out, wg_out,
    fb, pb, tb, ogb, nb, selfb, ftb, wt, tabv, tabs, inv_deg,
    ls, lr, cs, yr, ms, zr, zx, zy, sm,
    ga, bs, br, gs, gacc,
    pw, rc, x1, rx, xs, y1, ry, yt, yg,
    loc_sem, f_s, f_r, px_s, px_r, py_s, py_r, pc_s, pc_r, l_s, l_r,
    yf_s, yf_r, zf_s, zf_r, zx_s, zx_r, zy_s, zy_r, ag_s, ag_r, yb_s, yb_r,
    rc_s, rc_r, rx_s, rx_r, ry_s, ry_r, yg_s, yg_r,
):
    d = lax.axis_index("dom")
    f = lax.axis_index("feat")
    y, z = d // NZ, d % NZ
    x, c = f // NC, f % NC

    def to_feat(g):
        return (d, g)

    def to_yz(yy, zz):
        return (yy * NZ + zz, f)

    def remote(a, b, s, r, dev):
        return pltpu.make_async_remote_copy(
            src_ref=a, dst_ref=b, send_sem=s, recv_sem=r, device_id=dev, device_id_type=MESH
        )

    own_f = pltpu.make_async_copy(feats.at[f], fb.at[f], loc_sem.at[0])
    own_p = pltpu.make_async_copy(proj, pb.at[x, c], loc_sem.at[1])
    own_t = pltpu.make_async_copy(tiles, tb, loc_sem.at[2])
    own_g = pltpu.make_async_copy(out_grad, ogb, loc_sem.at[3])
    own_f.start()
    own_p.start()

    barrier = pltpu.get_barrier_semaphore()
    for o in range(1, NF):
        pl.semaphore_signal(barrier, inc=1, device_id=to_feat((f + o) % NF), device_id_type=MESH)
    for o in range(1, NY):
        pl.semaphore_signal(barrier, inc=1, device_id=to_yz((y + o) % NY, z), device_id_type=MESH)
    for o in (1, 2, NZ - 2, NZ - 1):
        pl.semaphore_signal(barrier, inc=1, device_id=to_yz(y, (z + o) % NZ), device_id_type=MESH)
    pl.semaphore_wait(barrier, NF + NY + 2)

    def f_copy(ox, oc):
        g = ((x + ox) % NX) * NC + (c + oc) % NC
        back = ((NX - ox) % NX) * NC + oc
        return remote(feats.at[g], fb.at[f], f_s.at[ox * NC + oc], f_r.at[back], to_feat(g))

    sibling = to_feat(x * NC + 1 - c)
    quarter = pl.ds(pl.multiple_of(y * (BLK // NY), BLK // NY), BLK // NY)

    def px_copy(o):
        return remote(
            proj.at[quarter], pb.at[x, c, quarter], px_s.at[o], px_r.at[NX - o],
            to_feat(((x + o) % NX) * NC + c),
        )

    def py_copy(o, oy):
        piece = pb.at[(x + o) % NX, c, quarter]
        return remote(
            piece, piece, py_s.at[o, oy], py_r.at[o, NY - oy], to_yz((y + oy) % NY, z)
        )

    def pc_copy(o):
        shard = pb.at[(x + o) % NX, c]
        return remote(shard if o else proj, shard, pc_s.at[o], pc_r.at[o], sibling)

    for o in (2, 1, 3):
        px_copy(o).start()
    for ox, oc in FAR_FIRST:
        f_copy(ox, oc).start()
    pc_copy(0).start()
    own_t.start()
    own_g.start()

    o_at = lax.broadcasted_iota(jnp.int32, (ND, SLOTS), 0)
    s_at = lax.broadcasted_iota(jnp.int32, (ND, SLOTS), 1)
    named = owner[...] == o_at
    before = jnp.dot(
        named.astype(BF), (o_at < s_at).astype(BF), preferred_element_type=F32
    )
    lane = lax.broadcasted_iota(jnp.int32, (ND, 128), 1)
    for i in range(CAP):
        here = named & (before == float(i))
        slot = jnp.sum(jnp.where(here, s_at.astype(F32), 0.0), axis=1, keepdims=True)
        label = jnp.sum(
            jnp.where(here, block[...].astype(F32) + 1.0, 0.0), axis=1, keepdims=True
        )
        tabv[i] = jnp.where(lane == 0, slot, 0.0).astype(jnp.int32)
        rows = jnp.broadcast_to((label - 1.0).astype(jnp.int32), (ND, HID))
        ls[:, i] = rows.reshape(NY, NZ, HID)
    picks = jnp.zeros((SLOTS, 128), F32)
    for k in range(KB):
        column = jnp.sum(
            jnp.where(o_at == s_at, source[k : k + 1, :].astype(F32), 0.0), axis=1, keepdims=True
        )
        picks = picks + jnp.where(lane == k, column, 0.0)
    tabv[CAP] = picks.astype(jnp.int32)
    table = pltpu.make_async_copy(tabv, tabs, loc_sem.at[4])
    table.start()

    def l_copy(o):
        yy = (y + o) % NY
        return remote(ls.at[yy], lr.at[NY - o], l_s.at[o], l_r.at[NY - o], to_yz(yy, z))

    for o in range(1, NY):
        l_copy(o).start()
    lr[0] = ls[y]

    for o in (1, 3, 2):
        piece = pb.at[(x + o) % NX, c, quarter]
        pltpu.make_async_copy(piece, piece, px_r.at[o]).wait()
        for oy in range(1, NY):
            py_copy(o, oy).start()

    diagonal = lax.broadcasted_iota(jnp.int32, (BLK, BLK), 0) == lax.broadcasted_iota(
        jnp.int32, (BLK, BLK), 1
    )
    for b in range(NB):
        column = jnp.sum(
            jnp.where(diagonal, counts[b : b + 1, :].astype(F32), 0.0), axis=1, keepdims=True
        )
        inv_deg[b * BLK : (b + 1) * BLK, :] = jnp.broadcast_to(1.0 / column, (BLK, HID))

    own_p.wait()
    for o in (1, 3, 2):
        for oy in range(1, NY):
            theirs = pl.ds(pl.multiple_of(((y + oy) % NY) * (BLK // NY), BLK // NY), BLK // NY)
            piece = pb.at[(x + o) % NX, c, theirs]
            pltpu.make_async_copy(piece, piece, py_r.at[o, oy]).wait()
        pc_copy(o).start()
    table.wait()

    own_f.wait()
    sm[...] = jnp.dot(fb[f], pb[x, c, :, :HID], preferred_element_type=F32)
    for ox, oc in ARRIVAL:
        xx, cc = (x + ox) % NX, (c + oc) % NC
        g = xx * NC + cc
        if oc:
            shard = pb.at[xx, cc]
            pltpu.make_async_copy(shard, shard, pc_r.at[ox]).wait()
        pltpu.make_async_copy(fb.at[g], fb.at[g], f_r.at[ox * NC + oc]).wait()
        sm[...] += jnp.dot(fb[g], pb[xx, cc, :, :HID], preferred_element_type=F32)
    nb[...] = sm[...].astype(BF).reshape(NB, BLK, HID)
    own_t.wait()

    def far_first(t):
        return (z + NZ // 2 + (1 - 2 * (t % 2)) * ((t + 1) // 2)) % NZ

    def near_first(q):
        return (z + NZ + (1 - 2 * (q % 2)) * ((q + 1) // 2)) % NZ

    def yf_copy(t, o):
        return remote(
            cs.at[t, o], yr.at[t, NY - o], yf_s.at[t, o], yf_r.at[t, NY - o], to_yz((y + o) % NY, z)
        )

    def slot_at(i, at):
        return jnp.clip(tabs[i, at, 0], 0, SLOTS - 1)

    def source_at(s, k):
        return jnp.clip(tabs[CAP, s, k], 0, NB - 1)

    def contribute(t, carry):
        zz = far_first(t)
        for r in (2, 1, 3, 0):
            yy = (y + r) % NY
            for i in range(CAP):
                s = slot_at(i, yy * NZ + zz)
                total = None
                for k in range(0, KB, 2):
                    left = jnp.concatenate([tb[s, k], tb[s, k + 1]], axis=1)
                    right = jnp.concatenate(
                        [nb[source_at(s, k)], nb[source_at(s, k + 1)]], axis=0
                    )
                    part = jnp.dot(left, right, preferred_element_type=F32)
                    total = part if total is None else total + part
                if r:
                    cs[t, r, i] = total.astype(BF)
                else:
                    yr[t, 0, i] = total.astype(BF)
            if r:
                yf_copy(t, r).start()
        return carry

    lax.fori_loop(0, NZ, contribute, 0)

    sm[...] = jnp.dot(fb[f], pb[x, c, :, HID:], preferred_element_type=F32)
    for ox, oc in ARRIVAL:
        xx, cc = (x + ox) % NX, (c + oc) % NC
        sm[...] += jnp.dot(fb[xx * NC + cc], pb[xx, cc, :, HID:], preferred_element_type=F32)
    selfb[...] = sm[...].astype(BF)
    for o in range(1, NY):
        pltpu.make_async_copy(lr.at[o], lr.at[o], l_r.at[o]).wait()

    def along_z(o):
        return to_yz(y, (z + o + NZ) % NZ)

    def zf_copy(t):
        return remote(ms.at[t], zr.at[t], zf_s.at[t], zf_r.at[t], along_z({3: 2, 4: -2, 5: 1, 6: -1}[t]))

    def zx_copy(way):
        half = ms.at[0, pl.ds(2 * way, 2)]
        return remote(half, zx.at[way], zx_s.at[way], zx_r.at[way], along_z((2, -2)[way]))

    def zy_copy(way):
        return remote(ms.at[1 + way], zy.at[way], zy_s.at[way], zy_r.at[way], along_z((1, -1)[way]))

    def merge(t):
        zz = far_first(t)
        for o in range(1, NY):
            pltpu.make_async_copy(yr.at[t, o], yr.at[t, o], yf_r.at[t, o]).wait()
        way = t - 3
        if way in (0, 1):
            zx_copy(way).wait_recv()
            zy_copy(way).wait_recv()

        def rows(n, inner):
            part = pl.ds(pl.multiple_of(n * 32, 32), 32)
            sums = [jnp.zeros((32, HID), F32) for b in range(NB)]
            for o in range(NY):
                for i in range(CAP):
                    row = jnp.broadcast_to(lr[o, i, pl.ds(zz, 1), :], (32, HID))
                    value = yr[t, o, i, part, :].astype(F32)
                    for b in range(NB):
                        sums[b] = sums[b] + jnp.where(row == b, value, 0.0)
            for b in range(NB):
                if way in (0, 1):
                    sums[b] = sums[b] + zy[way, b, part, :].astype(F32)
                    if b // 2 == way:
                        sums[b] = sums[b] + zx[way, b % 2, part, :].astype(F32)
                if t < NZ - 1:
                    ms[t, b, part, :] = sums[b].astype(BF)
                else:
                    sm[pl.ds(pl.multiple_of(b * BLK + n * 32, 32), 32), :] = sums[b]
            return inner

        lax.fori_loop(0, BLK // 32, rows, 0)
        if t == 0:
            zx_copy(0).start()
            zx_copy(1).start()
        elif t < 3:
            zy_copy(t - 1).start()
        elif t < NZ - 1:
            zf_copy(t).start()

        def turn(n, inner):
            s = t * (SLOTS // (NZ - 1)) + n
            parts = [tb[s, k].astype(F32) for k in range(KB)]
            for b in range(NB):
                total = jnp.zeros((BLK, BLK), F32)
                for k in range(KB):
                    total = total + jnp.where(source_at(s, k) == b, parts[k], 0.0)
                wt[s, pl.ds(b * BLK, BLK), :] = total.astype(BF).T
            return inner

        if t < NZ - 1:
            most = SLOTS // (NZ - 1)
            lax.fori_loop(0, most if t < NZ - 2 else SLOTS - t * most, turn, 0)
            for g in (t, NZ - 1) if t == NZ - 2 else (t,):
                for b in range(NB):
                    ftb[g % NC, g // NC, :, pl.ds(b * BLK, BLK)] = fb[g, pl.ds(b * BLK, BLK), :].T

    for t in range(NZ):
        merge(t)
    own_g.wait()

    for t in range(3, NZ - 1):
        pltpu.make_async_copy(zr.at[t], zr.at[t], zf_r.at[t]).wait()

        def add(b, inner):
            rows = pl.ds(pl.multiple_of(b * BLK, BLK), BLK)
            sm[rows, :] = sm[rows, :] + zr[t, b].astype(F32)
            return inner

        lax.fori_loop(0, NB, add, 0)

    def pointwise(u):
        def some(n, carry):
            b, m = n // 2, n % 2
            rows = pl.ds(pl.multiple_of(b * BLK + u * HALF + m * 32, 32), 32)
            inv = inv_deg[rows, :]
            preact = sm[rows, :] * inv + selfb[rows, :].astype(F32)
            sigma = jax.nn.sigmoid(preact)
            act_out[rows, :] = (preact * sigma).astype(BF)
            grad_pre = ogb[rows, :].astype(F32) * sigma * (1.0 + preact * (1.0 - sigma))
            gs[rows, :] = grad_pre.astype(BF)
            ga[0, b, u, pl.ds(pl.multiple_of(m * 32, 32), 32), :] = (grad_pre * inv).astype(BF)
            return carry

        lax.fori_loop(0, NB * 2, some, 0)

    up, down = to_yz(y, (z + 1) % NZ), to_yz(y, (z + NZ - 1) % NZ)

    def ag_copy(k, way, u):
        q = 2 * k - 1 + way if k else 0
        blocks = pl.ds(0, NB) if k < NZ // 2 - 1 else pl.ds(2 * way, 2)
        to = 2 * k + 1 + way if k < NZ // 2 - 1 else NZ - 1
        return remote(
            ga.at[q, blocks, u], ga.at[to, blocks, u],
            ag_s.at[2 * k + way, u], ag_r.at[2 * k + way, u], (up, down)[way],
        )

    def yb_copy(q, o, u):
        return remote(
            bs.at[q, o, :, u], br.at[q, NY - o, :, u], yb_s.at[q, o, u], yb_r.at[q, NY - o, u],
            to_yz((y + o) % NY, z),
        )

    def answer(q, u):
        zz = near_first(q)

        def rows(n, inner):
            part = pl.ds(pl.multiple_of(n * 32, 32), 32)
            blocks = [ga[q, b, u, part, :].astype(F32) for b in range(NB)]
            for o in range(NY):
                for i in range(CAP):
                    row = jnp.broadcast_to(lr[o, i, pl.ds(zz, 1), :], (32, HID))
                    value = jnp.zeros((32, HID), F32)
                    for b in range(NB):
                        value = jnp.where(row == b, blocks[b], value)
                    if o:
                        bs[q, o, i, u, part, :] = value.astype(BF)
                    else:
                        br[q, 0, i, u, part, :] = value.astype(BF)
            return inner

        lax.fori_loop(0, HALF // 32, rows, 0)
        for o in (2, 1, 3):
            yb_copy(q, o, u).start()

    def backward(q):
        zz = near_first(q)
        for o in range(1, NY):
            for u in range(2):
                piece = br.at[q, o, :, u]
                pltpu.make_async_copy(piece, piece, yb_r.at[q, o, u]).wait()

        def pair(r, carry):
            at = ((y + r) % NY) * NZ + zz
            left = jnp.concatenate([wt[slot_at(0, at)], wt[slot_at(1, at)]], axis=1)
            right = br[q, r].reshape(CAP * BLK, HID)
            gacc[...] += jnp.dot(left, right, preferred_element_type=F32)
            return carry

        lax.fori_loop(0, NY, pair, 0)

    def rc_copy(h, o):
        xx = (x + o) % NX
        return remote(pw.at[h, xx], rc.at[h, xx], rc_s.at[h, o], rc_r.at[h, o], sibling)

    def rx_copy(h, o):
        xx = (x + o) % NX
        return remote(
            xs.at[h, xx], rx.at[h, NX - o], rx_s.at[h, o], rx_r.at[h, NX - o], to_feat(xx * NC + c)
        )

    def plane_copies(a, b, s, r, h, per_device):
        for oy, oz in PLANE:
            e = ((y + oy) % NY) * NZ + (z + oz) % NZ
            back = ((NY - oy) % NY) * NZ + (NZ - oz) % NZ
            part = a.at[h, e] if per_device else a.at[h]
            remote(part, b.at[h, back], s.at[h], r.at[h], (e, f)).start()

    def red_0(h, grad):
        def term(parity):
            left = ftb[parity].reshape(NX * BLK, ROWS)
            return jnp.dot(left, grad, preferred_element_type=F32).reshape(NX, BLK, HID)

        pw[h] = term(1 - c)
        for o in (2, 1, 3, 0):
            rc_copy(h, o).start()
        x1[h] = term(c)

    def red_1(h):
        for o in (2, 1, 3, 0):
            xx = (x + o) % NX
            rc_copy(h, o).wait_recv()
            x1[h, xx] = x1[h, xx] + rc[h, xx]
            if o:
                xs[h, xx] = x1[h, xx].astype(BF)
                rx_copy(h, o).start()

    def red_2(h):
        total = x1[h, x]
        for o in (1, 3, 2):
            pltpu.make_async_copy(rx.at[h, o], rx.at[h, o], rx_r.at[h, o]).wait()
            total = total + rx[h, o].astype(F32)
        for n in range(ND):
            r, q = n // 2, n % 2
            y1[h, n] = total[r * 8 : r * 8 + 8, q * 128 : q * 128 + 128]

    def red_3(h):
        plane_copies(y1, ry, ry_s, ry_r, h, True)

    def others(buf, h):
        return buf.at[h, pl.ds(1, ND - 1)]

    def red_4(h):
        total = y1[h, d]
        pltpu.make_async_copy(others(ry, h), others(ry, h), ry_r.at[h]).wait()
        for o in range(1, ND):
            total = total + ry[h, o]
        yt[h] = total
        yg[h, 0] = total
        plane_copies(yt, yg, yg_s, yg_r, h, False)

    def red_5(h):
        pltpu.make_async_copy(others(yg, h), others(yg, h), yg_r.at[h]).wait()
        for n in range(ND):
            r, q = n // 2, n % 2
            back = ((n // NZ - y + NY) % NY) * NZ + (n % NZ - z + NZ) % NZ
            wg_out[pl.ds(r * 8, 8), pl.ds(HID * (1 - h) + q * 128, 128)] = yg[h, back]

    gacc[...] = jnp.zeros_like(gacc)
    for u in range(2):
        pointwise(u)
        for way in range(2):
            ag_copy(0, way, u).start()
        answer(0, u)

    def pass_on(k):
        for u in range(2):
            for way in range(2):
                ag_copy(k - 1, way, u).wait_recv()
                if k < NZ // 2:
                    ag_copy(k, way, u).start()
            if k < NZ // 2:
                answer(2 * k - 1, u)
                answer(2 * k, u)
            else:
                answer(NZ - 1, u)

    red_0(0, gs[...])
    pass_on(1)
    red_1(0)
    backward(0)
    pass_on(2)
    red_2(0)
    backward(1)
    pass_on(3)
    backward(2)
    pass_on(4)
    backward(3)
    for q in range(4, NZ):
        backward(q)

    grad = gacc[...].astype(BF)
    red_0(1, grad)
    red_1(1)
    red_3(0)
    red_2(1)
    red_3(1)
    red_4(0)
    red_4(1)
    red_5(0)
    red_5(1)

    for ox, oc in FAR_FIRST:
        f_copy(ox, oc).wait_send()
    for o in range(1, NX):
        px_copy(o).wait_send()
        for oy in range(1, NY):
            py_copy(o, oy).wait_send()
    for o in range(NX):
        pc_copy(o).wait_send()
    for o in range(1, NY):
        l_copy(o).wait_send()
    for t in range(NZ):
        for o in range(1, NY):
            yf_copy(t, o).wait_send()
            for u in range(2):
                yb_copy(t, o, u).wait_send()
        if 3 <= t < NZ - 1:
            zf_copy(t).wait_send()
    for way in range(2):
        zx_copy(way).wait_send()
        zy_copy(way).wait_send()
        for k in range(NZ // 2):
            for u in range(2):
                ag_copy(k, way, u).wait_send()
    for h in range(2):
        for o in range(NX):
            rc_copy(h, o).wait_send()
        for o in range(1, NX):
            rx_copy(h, o).wait_send()
        for buf, sem in ((ry, ry_s), (yg, yg_s)):
            pltpu.make_async_copy(others(buf, h), others(buf, h), sem.at[h]).wait()


def local(feats, projection, tiles, slot_owner, slot_block, source_block, counts, out_grad):
    vmem = pl.BlockSpec(memory_space=pltpu.VMEM)
    hbm = pl.BlockSpec(memory_space=pl.ANY)
    dma = pltpu.SemaphoreType.DMA
    scratch = [
        pltpu.VMEM((NF, ROWS, BLK), BF),
        pltpu.VMEM((NX, NC, BLK, 2 * HID), BF),
        pltpu.VMEM((SLOTS, KB, BLK, BLK), BF),
        pltpu.VMEM((ROWS, HID), BF),
        pltpu.VMEM((NB, BLK, HID), BF),
        pltpu.VMEM((ROWS, HID), BF),
        pltpu.VMEM((NC, NX, BLK, ROWS), BF),
        pltpu.VMEM((SLOTS, NB * BLK, BLK), BF),
        pltpu.VMEM((CAP + 1, ND, 128), jnp.int32),
        pltpu.SMEM((CAP + 1, ND, 128), jnp.int32),
        pltpu.VMEM((ROWS, HID), F32),
        pltpu.VMEM((NY, CAP, NZ, HID), jnp.int32),
        pltpu.VMEM((NY, CAP, NZ, HID), jnp.int32),
        pltpu.VMEM((NZ, NY, CAP, BLK, HID), BF),
        pltpu.VMEM((NZ, NY, CAP, BLK, HID), BF),
        pltpu.VMEM((NZ, NB, BLK, HID), BF),
        pltpu.VMEM((NZ, NB, BLK, HID), BF),
        pltpu.VMEM((2, 2, BLK, HID), BF),
        pltpu.VMEM((2, NB, BLK, HID), BF),
        pltpu.VMEM((ROWS, HID), F32),
        pltpu.VMEM((NZ, NB, 2, HALF, HID), BF),
        pltpu.VMEM((NZ, NY, CAP, 2, HALF, HID), BF),
        pltpu.VMEM((NZ, NY, CAP, 2, HALF, HID), BF),
        pltpu.VMEM((ROWS, HID), BF),
        pltpu.VMEM((ROWS, HID), F32),
        pltpu.VMEM((2, NX, BLK, HID), F32),
        pltpu.VMEM((2, NX, BLK, HID), F32),
        pltpu.VMEM((2, NX, BLK, HID), F32),
        pltpu.VMEM((2, NX, BLK, HID), BF),
        pltpu.VMEM((2, NX, BLK, HID), BF),
        pltpu.VMEM((2, ND, 8, 128), F32),
        pltpu.VMEM((2, ND, 8, 128), F32),
        pltpu.VMEM((2, 8, 128), F32),
        pltpu.VMEM((2, ND, 8, 128), F32),
        dma((5,)),
        dma((NF,)), dma((NF,)), dma((NX,)), dma((NX,)), dma((NX, NY)), dma((NX, NY)),
        dma((NX,)), dma((NX,)), dma((NY,)), dma((NY,)),
        dma((NZ, NY)), dma((NZ, NY)), dma((NZ,)), dma((NZ,)), dma((2,)), dma((2,)), dma((2,)), dma((2,)),
        dma((NZ, 2)), dma((NZ, 2)), dma((NZ, NY, 2)), dma((NZ, NY, 2)),
        dma((2, NX)), dma((2, NX)), dma((2, NX)), dma((2, NX)),
        dma((2,)), dma((2,)), dma((2,)), dma((2,)),
    ]
    return pl.pallas_call(
        main_kernel,
        out_shape=(
            jax.ShapeDtypeStruct((ROWS, HID), BF),
            jax.ShapeDtypeStruct((BLK, 2 * HID), F32),
        ),
        in_specs=[vmem] * 4 + [hbm] * 4,
        out_specs=[vmem] * 2,
        scratch_shapes=scratch,
        compiler_params=pltpu.CompilerParams(
            collective_id=0, has_side_effects=True, vmem_limit_bytes=53 << 20
        ),
    )(
        *(
            pltpu.with_memory_space_constraint(array, pltpu.HBM)
            for array in (
                slot_owner.reshape(1, SLOTS),
                slot_block.reshape(1, SLOTS),
                source_block.T,
                counts.reshape(NB, BLK),
                feats.reshape(NF, ROWS, BLK),
                projection,
                tiles,
                out_grad,
            )
        )
    )


def solution(mesh):
    placed = (
        P("dom", "feat"),
        P("feat", None),
        P(("dom", "feat"), None, None, None),
        P(("dom", "feat"), None),
        P(("dom", "feat"), None),
        P(("dom", "feat"), None),
        P(("dom", "feat")),
        P(("dom", "feat"), None),
    )
    return jax.shard_map(
        local,
        mesh=mesh,
        in_specs=placed,
        out_specs=(P(("dom", "feat"), None), P("feat", None)),
        check_vma=False,
    )
```
